32 devices in a mesh: dp: 4 (over y, x), ctx: 8 (over z, core).
Axes of the slice: x: 2, y: 2, z: 4, core: 2. Of those that a mesh axis runs over, the one named last changes fastest.
Arguments:
- tokens: bfloat16 [4, 4, 1024, 576], P(None, 'dp', 'ctx'), may hold values from -6 to 6
- prefix: int32 [4, 4], P(None, 'dp'), may hold values from 102 to 512
- norm_attn: bfloat16 [576], P('ctx'), may hold values from 0.5 to 1.5
- w_query: bfloat16 [576, 576], P('dp', 'ctx'), may hold values from -0.25 to 0.25
- w_key: bfloat16 [576, 192], P('dp', 'ctx'), may hold values from -0.25 to 0.25
- w_value: bfloat16 [576, 192], P('dp', 'ctx'), may hold values from -0.25 to 0.25
- w_output: bfloat16 [576, 576], P('dp', 'ctx'), may hold values from -2 to 2
- norm_ffn: bfloat16 [576], P('ctx'), may hold values from 0.5 to 1.5
- w_gate: bfloat16 [576, 1536], P('dp', 'ctx'), may hold values from -0.25 to 0.25
- w_up: bfloat16 [576, 1536], P('dp', 'ctx'), may hold values from -0.25 to 0.25
- w_down: bfloat16 [1536, 576], P('dp', 'ctx'), may hold values from -0.15625 to 0.15625
- cotangent: bfloat16 [4, 4, 1024, 576], P(None, 'dp', 'ctx'), may hold values from -6 to 6
Outputs:
- block_output: bfloat16 [4, 4, 1024, 576], P(None, 'dp', 'ctx')
- input_grad: float32 [4, 4, 1024, 576], P(None, 'dp', 'ctx')
- grad_norm_attn: float32 [576], P('ctx')
- grad_query: float32 [576, 576], P('dp', 'ctx')
- grad_key: float32 [576, 192], P('dp', 'ctx')
- grad_value: float32 [576, 192], P('dp', 'ctx')
- grad_output: float32 [576, 576], P('dp', 'ctx')
- grad_norm_ffn: float32 [576], P('ctx')
- grad_gate: float32 [576, 1536], P('dp', 'ctx')
- grad_up: float32 [576, 1536], P('dp', 'ctx')
- grad_down: float32 [1536, 576], P('dp', 'ctx')
The draws below stay inside these ranges and needn't reach their ends.
All inputs are finite; a program needn't handle non-finite values.
Results may differ from the reference program's by a relative error of at most 0.03.
Values may be sent and summed in bfloat16 or wider, within the bound.
No kernel may reach another device: no remote copies, remote signals or barrier semaphores. Data moves between devices by JAX's collectives and lax.ppermute only.
A program may use at most 256 MiB of HBM per device.

```python
import math
import jax
import jax.numpy as jnp
from jax import lax

D = 576
H = 9
KV = 3
HD = 64
FF = 1536
MICRO = 4
SEQS = 4
LENGTH = 1024


def set_ends(entries, own_key, smallest, top_value):
    longest = entries.shape.index(max(entries.shape))
    spots = []
    for shift in (0, 1):
        where = [jax.random.randint(jax.random.fold_in(own_key, axis), (), 0, length) for axis, length in enumerate(entries.shape)]
        where[longest] = (where[longest] + shift) % entries.shape[longest]
        spots.append(tuple(where))
    return entries.at[spots[0]].set(smallest).at[spots[1]].set(top_value)


def block_levels(own_key, extent, cuts, smallest, top_value):
    level, own = 1.0, jax.random.fold_in(own_key, 6)
    for dim, parts in cuts:
        heights = jnp.exp(jax.random.uniform(jax.random.fold_in(own, dim), (parts,), jnp.float32, smallest / len(cuts), top_value / len(cuts)))
        level = level * jnp.repeat(heights, extent[dim] // parts).reshape([-1 if axis == dim else 1 for axis in range(len(extent))])
    return level


def bell_draw(key, extent, deviation, limit, pieces=(), held_as=jnp.bfloat16):
    values = jax.random.normal(key, extent, jnp.float32) * deviation
    if len(pieces) > 0:
        values = block_levels(key, extent, pieces, -0.22, 0.18) * values
    return jnp.clip(values, min=-limit, max=limit).astype(held_as)


def setup_inputs(seed: int = 0) -> dict:
    keys = jax.random.split(jax.random.key(seed), 13)
    tokens = bell_draw(keys[0], (MICRO, SEQS, LENGTH, D), 1.0, 6.0, ((1, 4), (2, 8)))
    prefix = set_ends(jax.random.randint(keys[1], (MICRO, SEQS), LENGTH // 10, LENGTH // 2 + 1), jax.random.fold_in(keys[1], 1), LENGTH // 10, (LENGTH // 2 + 1) - 1).astype(jnp.int32)
    norm_attn = jnp.clip(1.0 + 0.1 * jax.random.normal(keys[2], (D,), jnp.float32), 0.5, 1.5).astype(jnp.bfloat16)
    w_query = bell_draw(keys[3], (D, H * HD), D ** -0.5, 0.25, ((0, 4), (1, 8)))
    w_key = bell_draw(keys[4], (D, KV * HD), D ** -0.5, 0.25, ((0, 4), (1, 8)))
    w_value = bell_draw(keys[5], (D, KV * HD), D ** -0.5, 0.25, ((0, 4), (1, 8)))
    w_output = bell_draw(keys[6], (H * HD, D), (max(H * HD // 64, 1)) ** -0.5, 2.0, ((0, 4), (1, 8)))
    norm_ffn = jnp.clip(1.0 + 0.1 * jax.random.normal(keys[7], (D,), jnp.float32), 0.5, 1.5).astype(jnp.bfloat16)
    w_gate = bell_draw(keys[8], (D, FF), D ** -0.5, 0.25, ((0, 4), (1, 8)))
    w_up = bell_draw(keys[9], (D, FF), D ** -0.5, 0.25, ((0, 4), (1, 8)))
    w_down = bell_draw(keys[10], (FF, D), FF ** -0.5, 0.15625, ((0, 4), (1, 8)))
    cotangent = bell_draw(keys[11], (MICRO, SEQS, LENGTH, D), 1.0, 6.0, ((1, 4), (2, 8)))
    return dict(tokens=tokens, prefix=prefix, norm_attn=norm_attn, w_query=w_query, w_key=w_key, w_value=w_value, w_output=w_output, norm_ffn=norm_ffn, w_gate=w_gate, w_up=w_up, w_down=w_down, cotangent=cotangent)


@jax.custom_vjp
def low(v):
    return lax.optimization_barrier(v.astype(jnp.bfloat16)).astype(jnp.float32)

@jax.custom_vjp
def low_back(v):
    return v

def low_keep(v):
    return (low(v), None)

def low_pass(kept, grad):
    return (grad,)

def back_keep(v):
    return (v, None)

def back_low(kept, grad):
    return (low(grad),)
low.defvjp(low_keep, low_pass)
low_back.defvjp(back_keep, back_low)
EPSILON = 1e-05
NEGATIVE = -1e+30
PRECISE = lax.Precision.HIGHEST

def rotary_tables(positions):
    half_width = HD // 2
    frequency = jnp.exp(jnp.arange(half_width, dtype=jnp.float32) * (-2.0 * math.log(10000.0) / HD))
    angles = positions.astype(jnp.float32)[:, None] * frequency[None, :]
    return (jnp.cos(angles), jnp.sin(angles))

def rotate(tensor, cosine_table, sine_table):
    half_width = tensor.shape[-1] // 2
    first_half = tensor[..., :half_width]
    second_half = tensor[..., half_width:]
    cosine_part = cosine_table[:, None, :]
    sine_part = sine_table[:, None, :]
    return jnp.concatenate([first_half * cosine_part - second_half * sine_part, second_half * cosine_part + first_half * sine_part], -1)

def rms_scale(stream, gain):
    return stream * lax.rsqrt(lax.optimization_barrier(jnp.mean(stream * stream, -1, keepdims=True)) + EPSILON) * gain

def attend_rows(query_rows, row_positions, key_rows, value_rows, prefix_len, key_positions):
    row_count = query_rows.shape[0]
    grouped = query_rows.reshape(row_count, KV, H // KV, HD)
    scores = jnp.einsum('ckgd,nkd->kgcn', grouped, key_rows, precision=PRECISE) * HD ** (-0.5)
    scores = low_back(scores)
    allowed = (key_positions[None, :] <= row_positions[:, None]) | (key_positions[None, :] < prefix_len)
    scores = jnp.where(allowed[None, None], scores, NEGATIVE)
    row_max = lax.optimization_barrier(jnp.max(scores, -1, keepdims=True))
    exp_terms = jnp.exp(scores - row_max)
    probability = exp_terms / lax.optimization_barrier(jnp.sum(exp_terms, -1, keepdims=True))
    mixture = jnp.einsum('kgcn,nkd->ckgd', low(probability), value_rows, precision=PRECISE)
    return mixture.reshape(row_count, H * HD)

def apply_block(stream, params, cosine_table, sine_table, positions, prefix_len):
    norm_first, w_query, w_key, w_value, w_output, norm_second, w_gate, w_up, w_down = params
    length = stream.shape[0]
    normed = low(rms_scale(stream, norm_first))
    queries = low(rotate(low_back(jnp.dot(normed, w_query, precision=PRECISE)).reshape(length, H, HD), cosine_table, sine_table))
    key_rows = low(rotate(low_back(jnp.dot(normed, w_key, precision=PRECISE)).reshape(length, KV, HD), cosine_table, sine_table))
    value_rows = low(low_back(jnp.dot(normed, w_value, precision=PRECISE))).reshape(length, KV, HD)
    block_rows = min(512, length)

    def one_block(items):
        query_block, row_positions = items
        return attend_rows(query_block, row_positions, key_rows, value_rows, prefix_len, positions)
    attended = lax.map(jax.checkpoint(one_block), (queries.reshape(length // block_rows, block_rows, H, HD), positions.reshape(length // block_rows, block_rows)))
    attended = low(low_back(attended.reshape(length, H * HD)))
    middle = stream + low_back(jnp.dot(attended, w_output, precision=PRECISE))
    normed_second = low(rms_scale(middle, norm_second))
    gate_value = low_back(jnp.dot(normed_second, w_gate, precision=PRECISE))
    up_value = low_back(jnp.dot(normed_second, w_up, precision=PRECISE))
    hidden = low(jax.nn.silu(gate_value) * up_value)
    return middle + low_back(jnp.dot(hidden, w_down, precision=PRECISE))

def reference(tokens, prefix, norm_attn, w_query, w_key, w_value, w_output, norm_ffn, w_gate, w_up, w_down, cotangent):
    params = tuple((weight.astype(jnp.float32) for weight in (norm_attn, w_query, w_key, w_value, w_output, norm_ffn, w_gate, w_up, w_down)))
    positions = jnp.arange(LENGTH, dtype=jnp.int32)
    cosine_table, sine_table = rotary_tables(positions)
    flat_tokens = tokens.reshape(MICRO * SEQS, LENGTH, D)
    flat_upstream = cotangent.reshape(MICRO * SEQS, LENGTH, D)
    flat_prefix = prefix.reshape(MICRO * SEQS)

    def per_sequence(totals, items):
        sequence, upstream, prefix_len = items

        def forward(stream, weights):
            for layer_index in range(2):
                stream = apply_block(stream, weights, cosine_table, sine_table, positions, prefix_len)
            return stream
        result, pull = jax.vjp(forward, sequence.astype(jnp.float32), params)
        stream_grad, weight_grads = pull(upstream.astype(jnp.float32))
        totals = tuple((former + latter for former, latter in zip(totals, weight_grads)))
        return (totals, (result.astype(jnp.bfloat16), stream_grad))
    start = tuple((jnp.zeros_like(weight) for weight in params))
    totals, (outputs, input_grads) = lax.scan(per_sequence, start, (flat_tokens, flat_upstream, flat_prefix))
    return (outputs.reshape(tokens.shape), input_grads.reshape(tokens.shape), totals[0], totals[1], totals[2], totals[3], totals[4], totals[5], totals[6], totals[7], totals[8])
```

```python
import functools
import math

import jax
import jax.numpy as jnp
from jax import lax
from jax.experimental import pallas as pl
from jax.experimental.pallas import tpu as pltpu
from jax.sharding import PartitionSpec as P

H = 9
KV = 3
HD = 64
GRP = H // KV
EPSILON = 1e-05
NEGATIVE = -1e30
BF = jnp.bfloat16
F32 = jnp.float32
VMEM_LIMIT = 56 * 1024 * 1024


def dot(a, b, ca=1, cb=0):
    return lax.dot_general(a, b, (((ca,), (cb,)), ((), ())), preferred_element_type=F32)


def call(body, grid, in_specs, out_specs, out_shape, scratch=(), name=None):
    return pl.pallas_call(
        body,
        grid=grid,
        in_specs=in_specs,
        out_specs=out_specs,
        out_shape=out_shape,
        scratch_shapes=list(scratch),
        name=name,
        compiler_params=pltpu.CompilerParams(
            dimension_semantics=("arbitrary",) * len(grid), vmem_limit_bytes=VMEM_LIMIT
        ),
    )


def whole(shape):
    zeros = (0,) * len(shape)
    return pl.BlockSpec(shape, lambda *_: zeros)


def sds(shape, dtype):
    return jax.ShapeDtypeStruct(shape, dtype)


def norm_rows(h):
    return lax.rsqrt(jnp.mean(h * h, -1, keepdims=True) + EPSILON)


def half_swap(x, lane):
    return jnp.where(lane % HD < HD // 2, pltpu.roll(x, 96, 1), pltpu.roll(x, 32, 1))


def qkv_forward(h, gain, w, cs, sn):
    rows, width = h.shape

    def body(h_ref, g_ref, w_ref, cs_ref, sn_ref, na_ref, q_ref, kv_ref):
        x = h_ref[...].astype(F32)
        na = (x * norm_rows(x) * g_ref[...].astype(F32)).astype(BF)
        na_ref[...] = na
        y = dot(na, w_ref[...])
        lane = lax.broadcasted_iota(jnp.int32, (rows, 128), 1)
        low = lane < HD
        cosine = cs_ref[...]
        sine = sn_ref[...]
        turned = []
        for c in range((H + KV) // 2):
            x = y[:, 128 * c : 128 * c + 128]
            turned.append(x * cosine + half_swap(x, lane) * sine)
        for head in range(H):
            x = turned[head // 2] * (HD**-0.5)
            if head % 2:
                x = pltpu.roll(x, 64, 1)
            q_ref[head] = jnp.where(low, x, 0.0).astype(BF)
        base = (H + KV) * HD
        for j in range(KV):
            k = turned[(H + j) // 2]
            if (H + j) % 2:
                k = pltpu.roll(k, 64, 1)
            v = y[:, base + HD * j : base + HD * j + HD]
            kv_ref[j] = jnp.concatenate([k[:, :HD], v], axis=1).astype(BF)

    return call(
        body,
        (1,),
        [whole(h.shape), whole(gain.shape), whole(w.shape), whole(cs.shape), whole(sn.shape)],
        [whole((rows, width)), whole((H, rows, 128)), whole((KV, rows, 128))],
        [sds((rows, width), BF), sds((H, rows, 128), BF), sds((KV, rows, 128), BF)],
        name="qkv_forward",
    )(h, gain, w, cs, sn)


def key_bounds(slots, parts):
    return [max(parts * (s + 1), parts * slots // 2) for s in range(slots)]


def gather_keys(kv_refs, full_ref, slots, block):
    parts = len(kv_refs)
    for t in range(slots):
        for e in range(parts):
            start = (parts * t + e) * block
            full_ref[start : start + block, :] = kv_refs[e][0, t * block : t * block + block, :]


def attend_forward(q, kv_parts, meta, slots):
    parts = len(kv_parts)
    rows = q.shape[1]
    block = rows // slots
    bounds = key_bounds(slots, parts)

    def body(meta_ref, q_ref, *refs):
        kv_refs = refs[:parts]
        att_ref, linv_ref = refs[parts : parts + 2]
        p_refs = refs[parts + 2 : parts + 2 + slots]
        full_ref = refs[-1]
        gather_keys(kv_refs, full_ref, slots, block)
        prefix = meta_ref[0]
        lane = lax.broadcasted_iota(jnp.int32, (block, 128), 1)
        for s in range(slots):
            free = parts * s * block
            top = bounds[s] * block
            q_pos = (parts * s + meta_ref[1]) * block + lax.broadcasted_iota(
                jnp.int32, (block, block), 0
            )
            key_iota = lax.broadcasted_iota(jnp.int32, (block, block), 1)
            biases = []
            for t in range(s, bounds[s] // parts):
                for e in range(parts):
                    k_pos = (parts * t + meta_ref[1 + e]) * block + key_iota
                    biases.append(
                        jnp.where((k_pos <= q_pos) | (k_pos < prefix), 0.0, NEGATIVE)
                    )
            bias = jnp.concatenate(biases, axis=1)
            outs = []
            linvs = []
            for hh in range(GRP):
                qs = q_ref[hh, s * block : s * block + block, :]
                masked = dot(qs, full_ref[free:top, :], 1, 1) + bias
                top_score = jnp.max(masked, -1, keepdims=True)
                if free:
                    opened = dot(qs, full_ref[:free, :], 1, 1)
                    top_score = jnp.maximum(top_score, jnp.max(opened, -1, keepdims=True))
                term = jnp.exp(masked - top_score)
                total = jnp.sum(term, -1, keepdims=True)
                pb = term.astype(BF)
                p_refs[s][0, hh * block : hh * block + block, free:top] = pb
                mix = dot(pb, full_ref[free:top, :])
                if free:
                    term = jnp.exp(opened - top_score)
                    total = total + jnp.sum(term, -1, keepdims=True)
                    pb = term.astype(BF)
                    p_refs[s][0, hh * block : hh * block + block, :free] = pb
                    mix = mix + dot(pb, full_ref[:free, :])
                inverse = 1.0 / total
                outs.append((mix[:, HD:] * inverse).astype(BF))
                linvs.append(inverse)
            att_ref[0, s * block : s * block + block, :] = jnp.concatenate(outs, axis=1)
            packed = jnp.where(lane == 0, linvs[0], jnp.where(lane == 1, linvs[1], linvs[2]))
            linv_ref[0, s * block : s * block + block, :] = packed

    def head_block(shape):
        return pl.BlockSpec((1,) + shape, lambda j: (j,) + (0,) * len(shape))

    return call(
        body,
        (KV,),
        [
            pl.BlockSpec(memory_space=pltpu.SMEM),
            pl.BlockSpec((GRP, rows, 128), lambda j: (j, 0, 0)),
        ]
        + [head_block((rows, 128))] * parts,
        [head_block((rows, GRP * HD)), head_block((rows, 128))]
        + [head_block((GRP * block, b * block)) for b in bounds],
        [sds((KV, rows, GRP * HD), BF), sds((KV, rows, 128), F32)]
        + [sds((KV, GRP * block, b * block), BF) for b in bounds],
        [pltpu.VMEM((parts * rows, 128), BF)],
        name="attend_forward",
    )(meta, q, *kv_parts)


def attend_backward(q, kv_parts, datt, att, linv, probs, cs, sn, slots):
    parts = len(kv_parts)
    rows = q.shape[1]
    block = rows // slots
    bounds = key_bounds(slots, parts)
    total_keys = parts * rows

    def body(q_ref, datt_ref, att_ref, linv_ref, cs_ref, sn_ref, *refs):
        kv_refs = refs[:parts]
        p_refs = refs[parts : parts + slots]
        dq_ref = refs[parts + slots]
        dkv_refs = refs[parts + slots + 1 : parts + slots + 1 + parts]
        full_ref, acc_ref = refs[-2:]
        gather_keys(kv_refs, full_ref, slots, block)
        acc_ref[...] = jnp.zeros_like(acc_ref)
        lane = lax.broadcasted_iota(jnp.int32, (block, 128), 1)
        for s in range(slots):
            top = bounds[s] * block
            here = slice(s * block, s * block + block)
            keys = full_ref[:top, :]
            d_all = datt_ref[0, here, :].astype(F32)
            product = d_all * att_ref[0, here, :].astype(F32)
            dqs = []
            for hh in range(GRP):
                inverse = linv_ref[0, here, hh : hh + 1]
                cols = slice(hh * HD, hh * HD + HD)
                delta = jnp.sum(product[:, cols], -1, keepdims=True) * inverse
                scaled = (d_all[:, cols] * inverse).astype(BF)
                dpad = jnp.concatenate([jnp.zeros((block, HD), BF), scaled], axis=1)
                dp = dot(dpad, keys, 1, 1)
                pb = p_refs[s][0, hh * block : hh * block + block, :]
                ds = (pb.astype(F32) * (dp - delta)).astype(BF)
                dqs.append(dot(ds, keys))
                qs = q_ref[hh, here, :]
                acc_ref[:top, :] += dot(ds, qs, 0, 0) + dot(pb, dpad, 0, 0)
            cosine = cs_ref[here, :]
            sine = sn_ref[here, :]
            outs = []
            for x in dqs:
                x = x * (HD**-0.5)
                x = x * cosine - half_swap(x, lane) * sine
                outs.append(x[:, :HD].astype(BF))
            dq_ref[0, here, :] = jnp.concatenate(outs, axis=1)
        for t in range(slots):
            for e in range(parts):
                start = (parts * t + e) * block
                dkv_refs[e][0, t * block : t * block + block, :] = acc_ref[
                    start : start + block, :
                ].astype(BF)

    def head_block(shape):
        return pl.BlockSpec((1,) + shape, lambda j: (j,) + (0,) * len(shape))

    return call(
        body,
        (KV,),
        [
            pl.BlockSpec((GRP, rows, 128), lambda j: (j, 0, 0)),
            head_block((rows, GRP * HD)),
            head_block((rows, GRP * HD)),
            head_block((rows, 128)),
            whole(cs.shape),
            whole(sn.shape),
        ]
        + [head_block((rows, 128))] * parts
        + [head_block((GRP * block, b * block)) for b in bounds],
        [head_block((rows, GRP * HD))] + [head_block((rows, 128))] * parts,
        [sds((KV, rows, GRP * HD), BF)] + [sds((KV, rows, 128), BF)] * parts,
        [pltpu.VMEM((total_keys, 128), BF), pltpu.VMEM((total_keys, 128), F32)],
        name="attend_backward",
    )(q, datt, att, linv, cs, sn, *kv_parts, *probs)


def ffn_forward(h, att, w_out, gain, w_gate, w_up, w_down, last, width_f=512):
    rows, width = h.shape
    ff = w_gate.shape[1]
    steps = ff // width_f

    def body(h_ref, att_ref, wo_ref, g_ref, wg_ref, wu_ref, wd_ref, *refs):
        h1_ref, nb_ref, a_ref, b_ref, hid_ref, h2_ref = refs[:6]
        f = pl.program_id(0)

        @pl.when(f == 0)
        def _():
            h1 = h_ref[...].astype(F32)
            for j in range(KV):
                h1 = h1 + dot(att_ref[j], wo_ref[GRP * HD * j : GRP * HD * (j + 1), :])
            h1_ref[...] = h1
            h2_ref[...] = h1
            nb_ref[...] = (h1 * norm_rows(h1) * g_ref[...].astype(F32)).astype(BF)

        nb = nb_ref[...]
        gate = dot(nb, wg_ref[...])
        up = dot(nb, wu_ref[...])
        sig = 1.0 / (1.0 + jnp.exp(-gate))
        silu = gate * sig
        hid = (silu * up).astype(BF)
        hid_ref[...] = hid
        b_ref[...] = silu.astype(BF)
        a_ref[...] = (up * (sig + silu * (1.0 - sig))).astype(BF)
        h2_ref[...] += dot(hid, wd_ref[...])
        if last:

            @pl.when(f == steps - 1)
            def _():
                refs[6][...] = h2_ref[...].astype(BF)

    tall = pl.BlockSpec((width, width_f), lambda f: (0, f))
    acts = pl.BlockSpec((rows, width_f), lambda f: (0, f))
    out_specs = [whole((rows, width)), whole((rows, width)), acts, acts, acts, whole((rows, width))]
    out_shape = [
        sds((rows, width), F32),
        sds((rows, width), BF),
        sds((rows, ff), BF),
        sds((rows, ff), BF),
        sds((rows, ff), BF),
        sds((rows, width), F32),
    ]
    if last:
        out_specs.append(whole((rows, width)))
        out_shape.append(sds((rows, width), BF))
    return call(
        body,
        (steps,),
        [
            whole(h.shape),
            whole(att.shape),
            whole(w_out.shape),
            whole(gain.shape),
            tall,
            tall,
            pl.BlockSpec((width_f, width), lambda f: (f, 0)),
        ],
        out_specs,
        out_shape,
        name="ffn_forward",
    )(h, att, w_out, gain, w_gate, w_up, w_down)


def ffn_backward(g, kept, full, previous, width_f=256):
    h1, nb, a, b, hid, att = kept
    w_out, gain, w_gate, w_up, w_down = full
    rows, width = h1.shape
    ff = w_gate.shape[1]
    steps = ff // width_f
    final = previous is not None
    kind = BF if final else F32

    def body(*refs):
        g_ref, a_ref, b_ref, hid_ref, nb_ref, h1_ref, att_ref = refs[:7]
        gain_ref, wo_ref, wg_ref, wu_ref, wd_ref = refs[7:12]
        refs = refs[12:]
        if final:
            pd_ref, pg_ref, pu_ref, po_ref, pn_ref = refs[:5]
            refs = refs[5:]
        gd_ref, gg_ref, gu_ref, go_ref, gn_ref, g1_ref, datt_ref = refs[:7]
        nbt_ref, e2_ref, dnb_ref = refs[7:]
        f = pl.program_id(0)

        @pl.when(f == 0)
        def _():
            nbt_ref[...] = nb_ref[...].T
            e2_ref[...] = g_ref[...].astype(BF)
            dnb_ref[...] = jnp.zeros_like(dnb_ref)

        e2 = e2_ref[...]
        dh = dot(e2, wd_ref[...], 1, 1)
        dgate = (dh * a_ref[...].astype(F32)).astype(BF)
        dup = (dh * b_ref[...].astype(F32)).astype(BF)
        dnb_ref[...] += dot(dgate, wg_ref[...], 1, 1) + dot(dup, wu_ref[...], 1, 1)
        nbt = nbt_ref[...]
        gd = dot(hid_ref[...], e2, 0, 0)
        gg = dot(nbt, dgate)
        gu = dot(nbt, dup)
        if final:
            gd = gd + pd_ref[...]
            gg = gg + pg_ref[...]
            gu = gu + pu_ref[...]
        gd_ref[...] = gd.astype(kind)
        gg_ref[...] = gg.astype(kind)
        gu_ref[...] = gu.astype(kind)

        @pl.when(f == steps - 1)
        def _():
            h1v = h1_ref[...]
            r = norm_rows(h1v)
            dnb = dnb_ref[...]
            gn = jnp.sum(dnb * h1v * r, 0, keepdims=True)
            u = dnb * gain_ref[...].astype(F32)
            g1 = (
                g_ref[...].astype(F32)
                + r * u
                - h1v * (r * r * r * jnp.mean(u * h1v, -1, keepdims=True))
            )
            g1_ref[...] = g1
            e1 = g1.astype(BF)
            for j in range(KV):
                span = slice(GRP * HD * j, GRP * HD * (j + 1))
                datt_ref[j] = dot(e1, wo_ref[span, :], 1, 1).astype(BF)
                go = dot(att_ref[j], e1, 0, 0)
                if final:
                    go = go + po_ref[span, :]
                go_ref[span, :] = go.astype(kind)
            if final:
                gn = gn + pn_ref[...]
            gn_ref[...] = gn

    tall = pl.BlockSpec((width, width_f), lambda f: (0, f))
    acts = pl.BlockSpec((rows, width_f), lambda f: (0, f))
    flat = pl.BlockSpec((width_f, width), lambda f: (f, 0))
    one = whole((1, width))
    grads = [flat, tall, tall, whole((width, width)), one]
    return call(
        body,
        (steps,),
        [whole(g.shape), acts, acts, acts, whole(nb.shape), whole(h1.shape), whole(att.shape)]
        + [one, whole(w_out.shape), tall, tall, flat]
        + (grads if final else []),
        grads + [whole((rows, width)), whole((KV, rows, GRP * HD))],
        [
            sds((ff, width), kind),
            sds((width, ff), kind),
            sds((width, ff), kind),
            sds((width, width), kind),
            sds((1, width), F32),
            sds((rows, width), F32),
            sds((KV, rows, GRP * HD), BF),
        ],
        [
            pltpu.VMEM((width, rows), BF),
            pltpu.VMEM((rows, width), BF),
            pltpu.VMEM((rows, width), F32),
        ],
        name="ffn_backward",
    )(g, a, b, hid, nb, h1, att, gain, w_out, w_gate, w_up, w_down, *(previous or ()))


def qkv_backward(dq, dkv_parts, na, h, g1, gain, w, cs, sn, previous):
    rows, width = na.shape
    parts = len(dkv_parts)
    cols = w.shape[1]
    final = previous is not None
    kind = BF if final else F32

    def body(dq_ref, na_ref, h_ref, g1_ref, gain_ref, w_ref, cs_ref, sn_ref, *refs):
        dkv_refs = refs[:parts]
        refs = refs[parts:]
        if final:
            pw_ref, pn_ref = refs[:2]
            refs = refs[2:]
        gw_ref, gn_ref, g0_ref = refs
        lane = lax.broadcasted_iota(jnp.int32, (rows, 128), 1)
        cosine = cs_ref[...]
        sine = sn_ref[...]
        ks = []
        vs = []
        for j in range(KV):
            x = dkv_refs[0][j].astype(F32)
            for ref in dkv_refs[1:]:
                x = x + ref[j].astype(F32)
            k = x * cosine - half_swap(x, lane) * sine
            ks.append(k[:, :HD].astype(BF))
            vs.append(x[:, HD:].astype(BF))
        d = jnp.concatenate([dq_ref[j] for j in range(KV)] + ks + vs, axis=1)
        dna = dot(d, w_ref[...], 1, 1)
        gw = dot(na_ref[...], d, 0, 0)
        x = h_ref[...].astype(F32)
        r = norm_rows(x)
        gn = jnp.sum(dna * x * r, 0, keepdims=True)
        u = dna * gain_ref[...].astype(F32)
        g0_ref[...] = (
            g1_ref[...] + r * u - x * (r * r * r * jnp.mean(u * x, -1, keepdims=True))
        )
        if final:
            gw = gw + pw_ref[...]
            gn = gn + pn_ref[...]
        gw_ref[...] = gw.astype(kind)
        gn_ref[...] = gn

    args = [dq, na, h, g1, gain, w, cs, sn, *dkv_parts, *(previous or ())]
    return call(
        body,
        (1,),
        [whole(x.shape) for x in args],
        [whole((width, cols)), whole((1, width)), whole((rows, width))],
        [sds((width, cols), kind), sds((1, width), F32), sds((rows, width), F32)],
        name="qkv_backward",
    )(*args)


def shifted(total, group, step):
    pairs = []
    for i in range(total):
        z, c = divmod(i, group)
        pairs.append((i, ((z + step) % (total // group)) * group + c))
    return pairs


def within(total, group, step):
    return [(i, (i // group) * group + (i % group + step) % group) for i in range(total)]


def to_sequences(x, ctx, group):
    slots = x.shape[0]
    z = lax.axis_index("ctx") // group
    pieces = [lax.dynamic_index_in_dim(x, z, 0, keepdims=False)]
    for d in range(1, slots):
        piece = lax.dynamic_index_in_dim(x, (z + d) % slots, 0, keepdims=False)
        pieces.append(lax.ppermute(piece, "ctx", shifted(ctx, group, d)))
    out = jnp.stack(pieces)
    order = (z - jnp.arange(slots)) % slots
    return jnp.take(out, order, axis=0).reshape(slots * x.shape[1], x.shape[2])


def from_sequences(x, slots, ctx, group):
    rows = x.shape[0] // slots
    x = x.reshape(slots, rows, x.shape[1])
    z = lax.axis_index("ctx") // group
    pieces = [lax.dynamic_index_in_dim(x, z, 0, keepdims=False)]
    for d in range(1, slots):
        piece = lax.dynamic_index_in_dim(x, (z + d) % slots, 0, keepdims=False)
        pieces.append(lax.ppermute(piece, "ctx", shifted(ctx, group, d)))
    out = jnp.stack(pieces)
    order = (z - jnp.arange(slots)) % slots
    return jnp.take(out, order, axis=0)


def exchange(kv, ctx, group):
    return [kv] + [lax.ppermute(kv, "ctx", within(ctx, group, e)) for e in range(1, group)]


def exchange_back(parts, ctx, group):
    return [parts[0]] + [
        lax.ppermute(parts[e], "ctx", within(ctx, group, -e)) for e in range(1, group)
    ]


def tables(slots, block, group):
    c = lax.axis_index("ctx") % group
    half_width = HD // 2
    frequency = jnp.exp(jnp.arange(half_width, dtype=F32) * (-2.0 * math.log(10000.0) / HD))
    positions = (group * jnp.arange(slots)[:, None] + c) * block + jnp.arange(block)[None, :]
    angles = positions.reshape(-1).astype(F32)[:, None] * frequency[None, :]
    cosine, sine = jnp.cos(angles), jnp.sin(angles)
    return (
        jnp.concatenate([cosine] * 4, axis=1),
        jnp.concatenate([-sine, sine, -sine, sine], axis=1),
    )


def gather_matrix(shard):
    return lax.all_gather(
        lax.all_gather(shard, "ctx", axis=1, tiled=True), "dp", axis=0, tiled=True
    )


def scatter_matrix(grad):
    part = lax.psum_scatter(grad, "dp", scatter_dimension=0, tiled=True)
    return lax.psum_scatter(part, "ctx", scatter_dimension=1, tiled=True).astype(F32)


def body(
    tokens,
    prefix,
    norm_attn,
    w_query,
    w_key,
    w_value,
    w_output,
    norm_ffn,
    w_gate,
    w_up,
    w_down,
    cotangent,
):
    slots, _, block, width = tokens.shape
    ctx = lax.axis_size("ctx")
    group = ctx // slots
    index = lax.axis_index("ctx")
    c = index % group
    cs, sn = tables(slots, block, group)
    micro_prefix = lax.dynamic_index_in_dim(prefix[:, 0], index // group, 0, keepdims=True)
    members = (c - jnp.arange(group)) % group
    meta = jnp.concatenate([micro_prefix, members]).astype(jnp.int32)

    gains = lax.all_gather(jnp.stack([norm_attn, norm_ffn]), "ctx", axis=1, tiled=True)
    gain_attn, gain_ffn = gains[0:1], gains[1:2]
    w_qkv = jnp.concatenate(
        [gather_matrix(w_query), gather_matrix(w_key), gather_matrix(w_value)], axis=1
    )
    w_out = gather_matrix(w_output)
    full = (w_out, gain_ffn, gather_matrix(w_gate), gather_matrix(w_up), gather_matrix(w_down))

    h = to_sequences(tokens[:, 0], ctx, group)
    kept = []
    for layer in range(2):
        na, q, kv = qkv_forward(h, gain_attn, w_qkv, cs, sn)
        kv_parts = exchange(kv, ctx, group)
        att, linv, *probs = attend_forward(q, kv_parts, meta, slots)
        outs = ffn_forward(h, att, *full, layer == 1)
        h1, nb, a, b, hid, h2 = outs[:6]
        kept.append((h, na, q, kv_parts, att, linv, probs, h1, nb, a, b, hid))
        h = h2
    block_output = from_sequences(outs[6], slots, ctx, group)

    g = to_sequences(cotangent[:, 0], ctx, group)
    before_ffn = None
    before_qkv = None
    for layer in (1, 0):
        h, na, q, kv_parts, att, linv, probs, h1, nb, a, b, hid = kept[layer]
        *before_ffn, g1, datt = ffn_backward(g, (h1, nb, a, b, hid, att), full, before_ffn)
        dq, *dkv = attend_backward(q, kv_parts, datt, att, linv, probs, cs, sn, slots)
        dkv = exchange_back(dkv, ctx, group)
        *before_qkv, g = qkv_backward(
            dq, dkv, na, h, g1, gain_attn, w_qkv, cs, sn, before_qkv
        )
    input_grad = from_sequences(g.astype(BF), slots, ctx, group).astype(F32)
    grad_down, grad_gate, grad_up, grad_out, gn_ffn = before_ffn
    grad_qkv, gn_attn = before_qkv
    wq = H * HD
    wk = KV * HD
    gn = lax.psum(jnp.concatenate([gn_attn, gn_ffn], axis=0), "dp")
    gn = lax.psum_scatter(gn, "ctx", scatter_dimension=1, tiled=True)
    return (
        block_output[:, None],
        input_grad[:, None],
        gn[0],
        scatter_matrix(grad_qkv[:, :wq]),
        scatter_matrix(grad_qkv[:, wq : wq + wk]),
        scatter_matrix(grad_qkv[:, wq + wk :]),
        scatter_matrix(grad_out),
        gn[1],
        scatter_matrix(grad_gate),
        scatter_matrix(grad_up),
        scatter_matrix(grad_down),
    )


def solution(mesh):
    act = P(None, "dp", "ctx", None)
    mat = P("dp", "ctx")
    in_specs = (act, P(None, "dp"), P("ctx"), mat, mat, mat, mat, P("ctx"), mat, mat, mat, act)
    out_specs = (act, act, P("ctx"), mat, mat, mat, mat, P("ctx"), mat, mat, mat)
    return jax.shard_map(body, mesh=mesh, in_specs=in_specs, out_specs=out_specs, check_vma=False)
```

```python
import functools
import math

import jax
import jax.numpy as jnp
from jax import lax
from jax.experimental import pallas as pl
from jax.experimental.pallas import tpu as pltpu
from jax.sharding import PartitionSpec as P

H = 9
KV = 3
HD = 64
GRP = H // KV
EPSILON = 1e-05
NEGATIVE = -1e30
BF = jnp.bfloat16
F32 = jnp.float32
VMEM_LIMIT = 56 * 1024 * 1024


def dot(a, b, ca=1, cb=0):
    return lax.dot_general(a, b, (((ca,), (cb,)), ((), ())), preferred_element_type=F32)


def call(body, grid, in_specs, out_specs, out_shape, scratch=(), name=None):
    return pl.pallas_call(
        body,
        grid=grid,
        in_specs=in_specs,
        out_specs=out_specs,
        out_shape=out_shape,
        scratch_shapes=list(scratch),
        name=name,
        compiler_params=pltpu.CompilerParams(
            dimension_semantics=("arbitrary",) * len(grid), vmem_limit_bytes=VMEM_LIMIT
        ),
    )


def whole(shape):
    zeros = (0,) * len(shape)
    return pl.BlockSpec(shape, lambda *_: zeros)


def sds(shape, dtype):
    return jax.ShapeDtypeStruct(shape, dtype)


def norm_rows(h):
    return lax.rsqrt(jnp.mean(h * h, -1, keepdims=True) + EPSILON)


def half_swap(x, lane):
    return jnp.where(lane % HD < HD // 2, pltpu.roll(x, 96, 1), pltpu.roll(x, 32, 1))


def qkv_forward(h, gain, w, cs, sn):
    rows, width = h.shape

    def body(h_ref, g_ref, w_ref, cs_ref, sn_ref, na_ref, q_ref, kv_ref):
        x = h_ref[...].astype(F32)
        na = (x * norm_rows(x) * g_ref[0:1, :]).astype(BF)
        na_ref[...] = na
        y = dot(na, w_ref[...])
        lane = lax.broadcasted_iota(jnp.int32, (rows, 128), 1)
        low = lane < HD
        cosine = cs_ref[...]
        sine = sn_ref[...]
        turned = []
        for c in range((H + KV) // 2):
            x = y[:, 128 * c : 128 * c + 128]
            turned.append(x * cosine + half_swap(x, lane) * sine)
        for head in range(H):
            x = turned[head // 2] * (HD**-0.5)
            if head % 2:
                x = pltpu.roll(x, 64, 1)
            q_ref[head] = jnp.where(low, x, 0.0).astype(BF)
        base = (H + KV) * HD
        for j in range(KV):
            k = turned[(H + j) // 2]
            if (H + j) % 2:
                k = pltpu.roll(k, 64, 1)
            v = y[:, base + HD * j : base + HD * j + HD]
            kv_ref[j] = jnp.concatenate([k[:, :HD], v], axis=1).astype(BF)

    return call(
        body,
        (1,),
        [whole(h.shape), whole(gain.shape), whole(w.shape), whole(cs.shape), whole(sn.shape)],
        [whole((rows, width)), whole((H, rows, 128)), whole((KV, rows, 128))],
        [sds((rows, width), BF), sds((H, rows, 128), BF), sds((KV, rows, 128), BF)],
        name="qkv_forward",
    )(h, gain, w, cs, sn)


def key_bounds(slots, parts):
    return [max(parts * (s + 1), parts * slots // 2) for s in range(slots)]


def gather_keys(kv_refs, full_ref, slots, block):
    parts = len(kv_refs)
    for t in range(slots):
        for e in range(parts):
            start = (parts * t + e) * block
            full_ref[start : start + block, :] = kv_refs[e][0, t * block : t * block + block, :]


def attend_forward(q, kv_parts, meta, slots):
    parts = len(kv_parts)
    rows = q.shape[1]
    block = rows // slots
    bounds = key_bounds(slots, parts)

    def body(meta_ref, q_ref, *refs):
        kv_refs = refs[:parts]
        att_ref, linv_ref = refs[parts : parts + 2]
        p_refs = refs[parts + 2 : parts + 2 + slots]
        full_ref = refs[-1]
        gather_keys(kv_refs, full_ref, slots, block)
        prefix = meta_ref[0]
        lane = lax.broadcasted_iota(jnp.int32, (block, 128), 1)
        for s in range(slots):
            free = parts * s * block
            top = bounds[s] * block
            q_pos = (parts * s + meta_ref[1]) * block + lax.broadcasted_iota(
                jnp.int32, (block, block), 0
            )
            key_iota = lax.broadcasted_iota(jnp.int32, (block, block), 1)
            biases = []
            for t in range(s, bounds[s] // parts):
                for e in range(parts):
                    k_pos = (parts * t + meta_ref[1 + e]) * block + key_iota
                    biases.append(
                        jnp.where((k_pos <= q_pos) | (k_pos < prefix), 0.0, NEGATIVE)
                    )
            bias = jnp.concatenate(biases, axis=1)
            outs = []
            linvs = []
            for hh in range(GRP):
                qs = q_ref[hh, s * block : s * block + block, :]
                masked = dot(qs, full_ref[free:top, :], 1, 1) + bias
                top_score = jnp.max(masked, -1, keepdims=True)
                if free:
                    opened = dot(qs, full_ref[:free, :], 1, 1)
                    top_score = jnp.maximum(top_score, jnp.max(opened, -1, keepdims=True))
                term = jnp.exp(masked - top_score)
                total = jnp.sum(term, -1, keepdims=True)
                pb = term.astype(BF)
                p_refs[s][0, hh * block : hh * block + block, free:top] = pb
                mix = dot(pb, full_ref[free:top, :])
                if free:
                    term = jnp.exp(opened - top_score)
                    total = total + jnp.sum(term, -1, keepdims=True)
                    pb = term.astype(BF)
                    p_refs[s][0, hh * block : hh * block + block, :free] = pb
                    mix = mix + dot(pb, full_ref[:free, :])
                inverse = 1.0 / total
                outs.append((mix[:, HD:] * inverse).astype(BF))
                linvs.append(inverse)
            att_ref[0, s * block : s * block + block, :] = jnp.concatenate(outs, axis=1)
            packed = jnp.where(lane == 0, linvs[0], jnp.where(lane == 1, linvs[1], linvs[2]))
            linv_ref[0, s * block : s * block + block, :] = packed

    def head_block(shape):
        return pl.BlockSpec((1,) + shape, lambda j: (j,) + (0,) * len(shape))

    return call(
        body,
        (KV,),
        [
            pl.BlockSpec(memory_space=pltpu.SMEM),
            pl.BlockSpec((GRP, rows, 128), lambda j: (j, 0, 0)),
        ]
        + [head_block((rows, 128))] * parts,
        [head_block((rows, GRP * HD)), head_block((rows, 128))]
        + [head_block((GRP * block, b * block)) for b in bounds],
        [sds((KV, rows, GRP * HD), BF), sds((KV, rows, 128), F32)]
        + [sds((KV, GRP * block, b * block), BF) for b in bounds],
        [pltpu.VMEM((parts * rows, 128), BF)],
        name="attend_forward",
    )(meta, q, *kv_parts)


def attend_backward(q, kv_parts, datt, att, linv, probs, cs, sn, slots):
    parts = len(kv_parts)
    rows = q.shape[1]
    block = rows // slots
    bounds = key_bounds(slots, parts)
    total_keys = parts * rows

    def body(q_ref, datt_ref, att_ref, linv_ref, cs_ref, sn_ref, *refs):
        kv_refs = refs[:parts]
        p_refs = refs[parts : parts + slots]
        dq_ref = refs[parts + slots]
        dkv_refs = refs[parts + slots + 1 : parts + slots + 1 + parts]
        full_ref, acc_ref = refs[-2:]
        gather_keys(kv_refs, full_ref, slots, block)
        acc_ref[...] = jnp.zeros_like(acc_ref)
        lane = lax.broadcasted_iota(jnp.int32, (block, 128), 1)
        for s in range(slots):
            top = bounds[s] * block
            here = slice(s * block, s * block + block)
            keys = full_ref[:top, :]
            d_all = datt_ref[0, here, :].astype(F32)
            product = d_all * att_ref[0, here, :].astype(F32)
            dqs = []
            for hh in range(GRP):
                inverse = linv_ref[0, here, hh : hh + 1]
                cols = slice(hh * HD, hh * HD + HD)
                delta = jnp.sum(product[:, cols], -1, keepdims=True) * inverse
                scaled = (d_all[:, cols] * inverse).astype(BF)
                dpad = jnp.concatenate([jnp.zeros((block, HD), BF), scaled], axis=1)
                dp = dot(dpad, keys, 1, 1)
                pb = p_refs[s][0, hh * block : hh * block + block, :]
                ds = (pb.astype(F32) * (dp - delta)).astype(BF)
                dqs.append(dot(ds, keys))
                qs = q_ref[hh, here, :]
                acc_ref[:top, :] += dot(ds, qs, 0, 0) + dot(pb, dpad, 0, 0)
            cosine = cs_ref[here, :]
            sine = sn_ref[here, :]
            outs = []
            for x in dqs:
                x = x * (HD**-0.5)
                x = x * cosine - half_swap(x, lane) * sine
                outs.append(x[:, :HD].astype(BF))
            dq_ref[0, here, :] = jnp.concatenate(outs, axis=1)
        for t in range(slots):
            for e in range(parts):
                start = (parts * t + e) * block
                dkv_refs[e][0, t * block : t * block + block, :] = acc_ref[
                    start : start + block, :
                ].astype(BF)

    def head_block(shape):
        return pl.BlockSpec((1,) + shape, lambda j: (j,) + (0,) * len(shape))

    return call(
        body,
        (KV,),
        [
            pl.BlockSpec((GRP, rows, 128), lambda j: (j, 0, 0)),
            head_block((rows, GRP * HD)),
            head_block((rows, GRP * HD)),
            head_block((rows, 128)),
            whole(cs.shape),
            whole(sn.shape),
        ]
        + [head_block((rows, 128))] * parts
        + [head_block((GRP * block, b * block)) for b in bounds],
        [head_block((rows, GRP * HD))] + [head_block((rows, 128))] * parts,
        [sds((KV, rows, GRP * HD), BF)] + [sds((KV, rows, 128), BF)] * parts,
        [pltpu.VMEM((total_keys, 128), BF), pltpu.VMEM((total_keys, 128), F32)],
        name="attend_backward",
    )(q, datt, att, linv, cs, sn, *kv_parts, *probs)


def ffn_forward(h, att, w_out, gain, w_gate, w_up, w_down, last, width_f=512):
    rows, width = h.shape
    ff = w_gate.shape[1]
    steps = ff // width_f

    def body(h_ref, att_ref, wo_ref, g_ref, wg_ref, wu_ref, wd_ref, *refs):
        h1_ref, nb_ref, a_ref, b_ref, hid_ref, h2_ref = refs[:6]
        f = pl.program_id(0)

        @pl.when(f == 0)
        def _():
            h1 = h_ref[...].astype(F32)
            for j in range(KV):
                h1 = h1 + dot(att_ref[j], wo_ref[GRP * HD * j : GRP * HD * (j + 1), :])
            h1_ref[...] = h1
            h2_ref[...] = h1
            nb_ref[...] = (h1 * norm_rows(h1) * g_ref[1:2, :]).astype(BF)

        nb = nb_ref[...]
        gate = dot(nb, wg_ref[...])
        up = dot(nb, wu_ref[...])
        sig = 1.0 / (1.0 + jnp.exp(-gate))
        silu = gate * sig
        hid = (silu * up).astype(BF)
        hid_ref[...] = hid
        b_ref[...] = silu.astype(BF)
        a_ref[...] = (up * (sig + silu * (1.0 - sig))).astype(BF)
        h2_ref[...] += dot(hid, wd_ref[...])
        if last:

            @pl.when(f == steps - 1)
            def _():
                refs[6][...] = h2_ref[...].astype(BF)

    tall = pl.BlockSpec((width, width_f), lambda f: (0, f))
    acts = pl.BlockSpec((rows, width_f), lambda f: (0, f))
    out_specs = [whole((rows, width)), whole((rows, width)), acts, acts, acts, whole((rows, width))]
    out_shape = [
        sds((rows, width), F32),
        sds((rows, width), BF),
        sds((rows, ff), BF),
        sds((rows, ff), BF),
        sds((rows, ff), BF),
        sds((rows, width), F32),
    ]
    if last:
        out_specs.append(whole((rows, width)))
        out_shape.append(sds((rows, width), BF))
    return call(
        body,
        (steps,),
        [
            whole(h.shape),
            whole(att.shape),
            whole(w_out.shape),
            whole(gain.shape),
            tall,
            tall,
            pl.BlockSpec((width_f, width), lambda f: (f, 0)),
        ],
        out_specs,
        out_shape,
        name="ffn_forward",
    )(h, att, w_out, gain, w_gate, w_up, w_down)


def ffn_backward(g, kept, full, previous, width_f=256):
    h1, nb, a, b, hid, att = kept
    w_out, gain, w_gate, w_up, w_down = full
    rows, width = h1.shape
    ff = w_gate.shape[1]
    steps = ff // width_f
    final = previous is not None
    kind = BF if final else F32

    def body(*refs):
        g_ref, a_ref, b_ref, hid_ref, nb_ref, h1_ref, att_ref = refs[:7]
        gain_ref, wo_ref, wg_ref, wu_ref, wd_ref = refs[7:12]
        refs = refs[12:]
        if final:
            pd_ref, pg_ref, pu_ref, po_ref, pn_ref = refs[:5]
            refs = refs[5:]
        gd_ref, gg_ref, gu_ref, go_ref, gn_ref, g1_ref, datt_ref = refs[:7]
        nbt_ref, e2_ref, dnb_ref = refs[7:]
        f = pl.program_id(0)

        @pl.when(f == 0)
        def _():
            nbt_ref[...] = nb_ref[...].T
            e2_ref[...] = g_ref[...].astype(BF)
            dnb_ref[...] = jnp.zeros_like(dnb_ref)

        e2 = e2_ref[...]
        dh = dot(e2, wd_ref[...], 1, 1)
        dgate = (dh * a_ref[...].astype(F32)).astype(BF)
        dup = (dh * b_ref[...].astype(F32)).astype(BF)
        dnb_ref[...] += dot(dgate, wg_ref[...], 1, 1) + dot(dup, wu_ref[...], 1, 1)
        nbt = nbt_ref[...]
        gd = dot(hid_ref[...], e2, 0, 0)
        gg = dot(nbt, dgate)
        gu = dot(nbt, dup)
        if final:
            gd = gd + pd_ref[...]
            gg = gg + pg_ref[...]
            gu = gu + pu_ref[...]
        gd_ref[...] = gd.astype(kind)
        gg_ref[...] = gg.astype(kind)
        gu_ref[...] = gu.astype(kind)

        @pl.when(f == steps - 1)
        def _():
            h1v = h1_ref[...]
            r = norm_rows(h1v)
            dnb = dnb_ref[...]
            gn = jnp.sum(dnb * h1v * r, 0, keepdims=True)
            u = dnb * gain_ref[1:2, :]
            g1 = (
                g_ref[...].astype(F32)
                + r * u
                - h1v * (r * r * r * jnp.mean(u * h1v, -1, keepdims=True))
            )
            g1_ref[...] = g1
            e1 = g1.astype(BF)
            for j in range(KV):
                span = slice(GRP * HD * j, GRP * HD * (j + 1))
                datt_ref[j] = dot(e1, wo_ref[span, :], 1, 1).astype(BF)
                go = dot(att_ref[j], e1, 0, 0)
                if final:
                    go = go + po_ref[span, :]
                go_ref[span, :] = go.astype(kind)
            if final:
                gn = gn + pn_ref[...]
            gn_ref[...] = gn

    tall = pl.BlockSpec((width, width_f), lambda f: (0, f))
    acts = pl.BlockSpec((rows, width_f), lambda f: (0, f))
    flat = pl.BlockSpec((width_f, width), lambda f: (f, 0))
    one = whole((1, width))
    grads = [flat, tall, tall, whole((width, width)), one]
    return call(
        body,
        (steps,),
        [whole(g.shape), acts, acts, acts, whole(nb.shape), whole(h1.shape), whole(att.shape)]
        + [whole(gain.shape), whole(w_out.shape), tall, tall, flat]
        + (grads if final else []),
        grads + [whole((rows, width)), whole((KV, rows, GRP * HD))],
        [
            sds((ff, width), kind),
            sds((width, ff), kind),
            sds((width, ff), kind),
            sds((width, width), kind),
            sds((1, width), F32),
            sds((rows, width), F32),
            sds((KV, rows, GRP * HD), BF),
        ],
        [
            pltpu.VMEM((width, rows), BF),
            pltpu.VMEM((rows, width), BF),
            pltpu.VMEM((rows, width), F32),
        ],
        name="ffn_backward",
    )(g, a, b, hid, nb, h1, att, gain, w_out, w_gate, w_up, w_down, *(previous or ()))


def qkv_backward(dq, dkv_parts, na, h, g1, gain, w, cs, sn, previous):
    rows, width = na.shape
    parts = len(dkv_parts)
    cols = w.shape[1]
    final = previous is not None
    kind = BF if final else F32

    def body(dq_ref, na_ref, h_ref, g1_ref, gain_ref, w_ref, cs_ref, sn_ref, *refs):
        dkv_refs = refs[:parts]
        refs = refs[parts:]
        if final:
            pw_ref, pn_ref = refs[:2]
            refs = refs[2:]
        gw_ref, gn_ref, g0_ref = refs
        lane = lax.broadcasted_iota(jnp.int32, (rows, 128), 1)
        cosine = cs_ref[...]
        sine = sn_ref[...]
        ks = []
        vs = []
        for j in range(KV):
            x = dkv_refs[0][j].astype(F32)
            for ref in dkv_refs[1:]:
                x = x + ref[j].astype(F32)
            k = x * cosine - half_swap(x, lane) * sine
            ks.append(k[:, :HD].astype(BF))
            vs.append(x[:, HD:].astype(BF))
        d = jnp.concatenate([dq_ref[j] for j in range(KV)] + ks + vs, axis=1)
        dna = dot(d, w_ref[...], 1, 1)
        gw = dot(na_ref[...], d, 0, 0)
        x = h_ref[...].astype(F32)
        r = norm_rows(x)
        gn = jnp.sum(dna * x * r, 0, keepdims=True)
        u = dna * gain_ref[0:1, :]
        g0_ref[...] = (
            g1_ref[...] + r * u - x * (r * r * r * jnp.mean(u * x, -1, keepdims=True))
        )
        if final:
            gw = gw + pw_ref[...]
            gn = gn + pn_ref[...]
        gw_ref[...] = gw.astype(kind)
        gn_ref[...] = gn

    args = [dq, na, h, g1, gain, w, cs, sn, *dkv_parts, *(previous or ())]
    return call(
        body,
        (1,),
        [whole(x.shape) for x in args],
        [whole((width, cols)), whole((1, width)), whole((rows, width))],
        [sds((width, cols), kind), sds((1, width), F32), sds((rows, width), F32)],
        name="qkv_backward",
    )(*args)


def shifted(total, group, step):
    pairs = []
    for i in range(total):
        z, c = divmod(i, group)
        pairs.append((i, ((z + step) % (total // group)) * group + c))
    return pairs


def within(total, group, step):
    return [(i, (i // group) * group + (i % group + step) % group) for i in range(total)]


WQ = H * HD
WK = KV * HD
COLS_A = (0, 72, 96, 120, 192)
ROWS_D = 144
TOP = 80
SMEM_SPEC = pl.BlockSpec(memory_space=pltpu.SMEM)


def pack_shards(shards):
    def body(wq, wk, wv, wo, wg, wu, wd, ga, gf, a_ref, f_ref):
        a_ref[:ROWS_D, :] = jnp.concatenate([wq[...], wk[...], wv[...], wo[...]], axis=1)
        row = lax.broadcasted_iota(jnp.int32, (16, 72), 0)
        ga_row = ga[...].astype(F32)
        gf_row = gf[...].astype(F32)
        gains = jnp.where(row == 0, ga_row, jnp.where(row == 1, gf_row, 0.0))
        a_ref[ROWS_D:, :] = jnp.concatenate([gains, jnp.zeros((16, 120), F32)], axis=1).astype(BF)
        f_ref[:, :384] = jnp.concatenate([wg[...], wu[...]], axis=1)
        down = jnp.concatenate([wd[128 * i : 128 * i + 128, :] for i in range(3)], axis=1)
        f_ref[:, 384:] = jnp.concatenate([down, jnp.zeros((16, 216), BF)], axis=0)

    return call(
        body,
        (1,),
        [whole(x.shape) for x in shards],
        [whole((160, 192)), whole((ROWS_D, 600))],
        [sds((160, 192), BF), sds((ROWS_D, 600), BF)],
        name="pack_shards",
    )(*shards)


def send(x, axis, pairs):
    return lax.ppermute(x, axis, pairs)


def cross(step, count):
    return [(i, i ^ step) for i in range(count)]


def spread_z(x):
    return jnp.stack([x] + [send(x, "ctx", shifted(8, 2, d)) for d in (1, 2, 3)])


def spread_attn(x):
    stack = spread_z(x)
    mine = [stack] + [send(stack, "dp", cross(r, 4)) for r in (1, 2, 3)]
    return mine + [send(m, "ctx", cross(1, 8)) for m in mine]


def spread_ffn(x):
    stack = spread_z(x)
    by_x = send(stack, "dp", cross(1, 4))
    by_y = send(stack, "dp", cross(2, 4))
    upper = send(by_x[:, :TOP], "dp", cross(2, 4))
    lower = send(by_y[:, TOP:], "dp", cross(1, 4))
    mine = [stack, by_x, by_y, upper, lower]
    return mine + [send(m, "ctx", cross(1, 8)) for m in mine]


def ordered(c, own, sibling):
    return jnp.where(c == 0, own, sibling), jnp.where(c == 0, sibling, own)


def assemble_attn(coords, arrays):
    def body(co, *refs):
        own, sib = refs[:4], refs[4:8]
        w_ref, o_ref, g_ref = refs[8:]
        j_own, z_own, c_own = co[0], co[1], co[2]
        for r in range(4):
            row = pl.multiple_of((j_own ^ r) * ROWS_D, 16)
            pieces = []
            for z in range(4):
                d = lax.rem(z_own - z + 4, 4)
                pieces.extend(ordered(c_own, own[r][d], sib[r][d]))
            groups = [
                jnp.concatenate([p[:ROWS_D, a:b] for p in pieces], axis=1)
                for a, b in zip(COLS_A[:-1], COLS_A[1:])
            ]
            w_ref[pl.ds(row, ROWS_D), :] = jnp.concatenate(groups[:3], axis=1)
            o_ref[pl.ds(row, ROWS_D), :] = groups[3]
            if r == 0:
                g_ref[...] = jnp.concatenate(
                    [p[ROWS_D:, :72].astype(F32) for p in pieces], axis=1
                )

    shapes = [((576, 960), BF), ((576, 576), BF), ((16, 576), F32)]
    return call(
        body,
        (1,),
        [SMEM_SPEC] + [whole(x.shape) for x in arrays],
        [whole(s) for s, _ in shapes],
        [sds(s, t) for s, t in shapes],
        name="assemble_attn",
    )(coords, *arrays)


def assemble_ffn(coords, arrays):
    def body(co, *refs):
        own, sib = refs[:5], refs[5:10]
        g_ref, u_ref, d_ref = refs[10:]
        j_own, z_own, c_own = co[0], co[1], co[2]

        def read(group, r, d, cols):
            if r < 3:
                return group[r][d, :, cols]
            return jnp.concatenate([group[3][d, :, cols], group[4][d, :, cols]], axis=0)

        for r in range(4):
            j = j_own ^ r
            row = pl.multiple_of(j * ROWS_D, 16)
            downs = []
            for z in range(4):
                d = lax.rem(z_own - z + 4, 4)
                here = slice(384 * z, 384 * z + 384)
                even, odd = ordered(
                    c_own, read(own, r, d, slice(0, 384)), read(sib, r, d, slice(0, 384))
                )
                g_ref[pl.ds(row, ROWS_D), here] = jnp.concatenate(
                    [even[:, :192], odd[:, :192]], axis=1
                )
                u_ref[pl.ds(row, ROWS_D), here] = jnp.concatenate(
                    [even[:, 192:], odd[:, 192:]], axis=1
                )
                downs.extend(
                    ordered(
                        c_own, read(own, r, d, slice(384, 600)), read(sib, r, d, slice(384, 600))
                    )
                )
            for i in range(3):
                row = pl.multiple_of(j * 384 + 128 * i, 128)
                d_ref[pl.ds(row, 128), :] = jnp.concatenate(
                    [p[:128, 72 * i : 72 * i + 72] for p in downs], axis=1
                )

    shapes = [((576, 1536), BF), ((576, 1536), BF), ((1536, 576), BF)]
    return call(
        body,
        (1,),
        [SMEM_SPEC] + [whole(x.shape) for x in arrays],
        [whole(s) for s, _ in shapes],
        [sds(s, t) for s, t in shapes],
        name="assemble_ffn",
    )(coords, *arrays)


def split_attn(coords, g_qkv, g_out, gn_attn, gn_ffn):
    def body(co, gw, go, ga, gf, *outs):
        keep, away = outs[:4], outs[4]
        j_own, z_own, c_own = co[0], co[1], co[2]
        bases = (0, WQ, WQ + WK)
        sub = lax.broadcasted_iota(jnp.int32, (16, 576), 0)
        gains = jnp.where(sub == 0, ga[...], jnp.where(sub == 1, gf[...], 0.0)).astype(BF)
        for r in range(4):
            row = pl.multiple_of((j_own ^ r) * ROWS_D, 16)
            wide = gw[pl.ds(row, ROWS_D), :]
            out = go[pl.ds(row, ROWS_D), :]
            for z in range(4):
                d = lax.rem(z - z_own + 4, 4)
                pair = []
                for k in (2 * z, 2 * z + 1):
                    top = jnp.concatenate(
                        [
                            wide[:, 72 * k : 72 * k + 72],
                            wide[:, WQ + 24 * k : WQ + 24 * k + 24],
                            wide[:, WQ + WK + 24 * k : WQ + WK + 24 * k + 24],
                            out[:, 72 * k : 72 * k + 72],
                        ],
                        axis=1,
                    )
                    low = jnp.concatenate(
                        [gains[:, 72 * k : 72 * k + 72], jnp.zeros((16, 120), BF)], axis=1
                    )
                    pair.append(jnp.concatenate([top, low], axis=0))
                mine, other = ordered(c_own, *pair)
                keep[r][d] = mine
                away[r, d] = other

    shapes = [(4, 160, 192)] * 4 + [(4, 4, 160, 192)]
    args = (g_qkv, g_out, gn_attn, gn_ffn)
    return call(
        body,
        (1,),
        [SMEM_SPEC] + [whole(x.shape) for x in args],
        [whole(s) for s in shapes],
        [sds(s, BF) for s in shapes],
        name="split_attn",
    )(coords, *args)


def split_ffn(coords, g_gate, g_up, g_down):
    def body(co, gg, gu, gd, *outs):
        keep, away = outs[:4], outs[4]
        j_own, z_own, c_own = co[0], co[1], co[2]
        for r in range(4):
            j = j_own ^ r
            row = pl.multiple_of(j * ROWS_D, 16)
            thirds = [
                gd[pl.ds(pl.multiple_of(j * 384 + 128 * i, 128), 128), :] for i in range(3)
            ]
            for z in range(4):
                d = lax.rem(z - z_own + 4, 4)
                gate = gg[pl.ds(row, ROWS_D), 384 * z : 384 * z + 384]
                up = gu[pl.ds(row, ROWS_D), 384 * z : 384 * z + 384]
                pair = []
                for i in range(2):
                    k = 2 * z + i
                    here = slice(192 * i, 192 * i + 192)
                    left = jnp.concatenate([gate[:, here], up[:, here]], axis=1)
                    right = jnp.concatenate([t[:, 72 * k : 72 * k + 72] for t in thirds], axis=1)
                    right = jnp.concatenate([right, jnp.zeros((16, 216), BF)], axis=0)
                    pair.append((left, right))
                for part, cols in ((0, slice(0, 384)), (1, slice(384, 600))):
                    mine, other = ordered(c_own, pair[0][part], pair[1][part])
                    keep[r][d, :, cols] = mine
                    away[r, d, :, cols] = other

    shapes = [(4, ROWS_D, 600)] * 4 + [(4, 4, ROWS_D, 600)]
    args = (g_gate, g_up, g_down)
    return call(
        body,
        (1,),
        [SMEM_SPEC] + [whole(x.shape) for x in args],
        [whole(s) for s in shapes],
        [sds(s, BF) for s in shapes],
        name="split_ffn",
    )(coords, *args)


def total(terms):
    out = terms[0].astype(F32)
    for t in terms[1:]:
        out = out + t.astype(F32)
    return out.astype(BF)


def gather_sums(pieces):
    keep, away = pieces[:4], pieces[4]
    back = send(away, "ctx", cross(1, 8))
    sums = [total([keep[r], back[r]]) for r in range(4)]
    mine = total([sums[0]] + [send(sums[r], "dp", cross(r, 4)) for r in (1, 2, 3)])
    return [mine[0]] + [send(mine[d], "ctx", shifted(8, 2, d)) for d in (1, 2, 3)]


def finish_attn(terms):
    def body(a, b, c, d, q_ref, k_ref, v_ref, o_ref, ga_ref, gf_ref):
        x = a[...].astype(F32) + b[...].astype(F32) + c[...].astype(F32) + d[...].astype(F32)
        for ref, lo, hi in zip((q_ref, k_ref, v_ref, o_ref), COLS_A[:-1], COLS_A[1:]):
            ref[...] = x[:ROWS_D, lo:hi]
        ga_ref[...] = x[ROWS_D : ROWS_D + 1, :72]
        gf_ref[...] = x[ROWS_D + 1 : ROWS_D + 2, :72]

    shapes = [(ROWS_D, b - a) for a, b in zip(COLS_A[:-1], COLS_A[1:])] + [(1, 72), (1, 72)]
    return call(
        body,
        (1,),
        [whole(x.shape) for x in terms],
        [whole(s) for s in shapes],
        [sds(s, F32) for s in shapes],
        name="finish_attn",
    )(*terms)


def finish_ffn(terms):
    def body(a, b, c, d, g_ref, u_ref, d_ref):
        x = a[...].astype(F32) + b[...].astype(F32) + c[...].astype(F32) + d[...].astype(F32)
        g_ref[...] = x[:, :192]
        u_ref[...] = x[:, 192:384]
        for i in range(3):
            d_ref[128 * i : 128 * i + 128, :] = x[:128, 384 + 72 * i : 456 + 72 * i]

    shapes = [(ROWS_D, 192), (ROWS_D, 192), (384, 72)]
    return call(
        body,
        (1,),
        [whole(x.shape) for x in terms],
        [whole(s) for s in shapes],
        [sds(s, F32) for s in shapes],
        name="finish_ffn",
    )(*terms)


def pick_slots(coords, x):
    slots, rows, width = x.shape

    def body(co, x_ref, *outs):
        for d in range(slots):
            outs[d][...] = x_ref[lax.rem(co[1] + d, slots)].astype(BF)

    return call(
        body,
        (1,),
        [SMEM_SPEC, whole(x.shape)],
        [whole((rows, width))] * slots,
        [sds((rows, width), BF)] * slots,
        name="pick_slots",
    )(coords, x)


def place_slots(coords, pieces, dtype):
    slots = len(pieces)
    rows, width = pieces[0].shape

    def body(co, *refs):
        for d in range(slots):
            refs[slots][lax.rem(co[1] - d + slots, slots)] = refs[d][...].astype(dtype)

    return call(
        body,
        (1,),
        [SMEM_SPEC] + [whole((rows, width))] * slots,
        [whole((slots, rows, width))],
        [sds((slots, rows, width), dtype)],
        name="place_slots",
    )(coords, *pieces)[0]


def redeal(coords, x, ctx, group, dtype=BF):
    pieces = pick_slots(coords, x)
    moved = [pieces[0]] + [
        lax.ppermute(pieces[d], "ctx", shifted(ctx, group, d)) for d in range(1, len(pieces))
    ]
    return place_slots(coords, moved, dtype)


def exchange(kv, ctx, group):
    return [kv] + [lax.ppermute(kv, "ctx", within(ctx, group, e)) for e in range(1, group)]


def exchange_back(parts, ctx, group):
    return [parts[0]] + [
        lax.ppermute(parts[e], "ctx", within(ctx, group, -e)) for e in range(1, group)
    ]


def tables(slots, block, group):
    c = lax.axis_index("ctx") % group
    half_width = HD // 2
    frequency = jnp.exp(jnp.arange(half_width, dtype=F32) * (-2.0 * math.log(10000.0) / HD))
    positions = (group * jnp.arange(slots)[:, None] + c) * block + jnp.arange(block)[None, :]
    angles = positions.reshape(-1).astype(F32)[:, None] * frequency[None, :]
    cosine, sine = jnp.cos(angles), jnp.sin(angles)
    return (
        jnp.concatenate([cosine] * 4, axis=1),
        jnp.concatenate([-sine, sine, -sine, sine], axis=1),
    )


def gather_matrix(shard):
    return lax.all_gather(
        lax.all_gather(shard, "ctx", axis=1, tiled=True), "dp", axis=0, tiled=True
    )


def scatter_matrix(grad):
    part = lax.psum_scatter(grad, "dp", scatter_dimension=0, tiled=True)
    return lax.psum_scatter(part, "ctx", scatter_dimension=1, tiled=True).astype(F32)


def body(
    tokens,
    prefix,
    norm_attn,
    w_query,
    w_key,
    w_value,
    w_output,
    norm_ffn,
    w_gate,
    w_up,
    w_down,
    cotangent,
):
    slots, _, block, width = tokens.shape
    ctx = lax.axis_size("ctx")
    group = ctx // slots
    index = lax.axis_index("ctx")
    c = index % group
    cs, sn = tables(slots, block, group)
    micro_prefix = lax.dynamic_index_in_dim(prefix[:, 0], index // group, 0, keepdims=True)
    members = (c - jnp.arange(group)) % group
    meta = jnp.concatenate([micro_prefix, members]).astype(jnp.int32)

    dp = lax.axis_size("dp")
    coords = jnp.stack([lax.axis_index("dp"), index // group, c]).astype(jnp.int32)
    tight = dp == 4 and ctx == 8 and slots == 4 and w_query.shape == (ROWS_D, 72)

    if tight:
        shards = (w_query, w_key, w_value, w_output, w_gate, w_up, w_down)
        pack_a, pack_f = pack_shards(shards + (norm_attn[None], norm_ffn[None]))
        w_qkv, w_out, gains = assemble_attn(coords, spread_attn(pack_a))
        w_ffn = assemble_ffn(coords, spread_ffn(pack_f))
    else:
        gains = lax.all_gather(jnp.stack([norm_attn, norm_ffn]), "ctx", axis=1, tiled=True)
        gains = jnp.concatenate([gains.astype(F32), jnp.zeros((14, width), F32)], axis=0)
        w_qkv = jnp.concatenate(
            [gather_matrix(w_query), gather_matrix(w_key), gather_matrix(w_value)], axis=1
        )
        w_out = gather_matrix(w_output)
        w_ffn = [gather_matrix(w_gate), gather_matrix(w_up), gather_matrix(w_down)]
    full = (w_out, gains, *w_ffn)

    h = redeal(coords, tokens[:, 0], ctx, group).reshape(slots * block, width)
    kept = []
    for layer in range(2):
        na, q, kv = qkv_forward(h, gains, w_qkv, cs, sn)
        kv_parts = exchange(kv, ctx, group)
        att, linv, *probs = attend_forward(q, kv_parts, meta, slots)
        outs = ffn_forward(h, att, *full, layer == 1)
        h1, nb, a, b, hid, h2 = outs[:6]
        kept.append((h, na, q, kv_parts, att, linv, probs, h1, nb, a, b, hid))
        h = h2
    block_output = redeal(coords, outs[6].reshape(slots, block, width), ctx, group)

    g = redeal(coords, cotangent[:, 0], ctx, group).reshape(slots * block, width)
    before_ffn = None
    before_qkv = None
    for layer in (1, 0):
        h, na, q, kv_parts, att, linv, probs, h1, nb, a, b, hid = kept[layer]
        *before_ffn, g1, datt = ffn_backward(g, (h1, nb, a, b, hid, att), full, before_ffn)
        dq, *dkv = attend_backward(q, kv_parts, datt, att, linv, probs, cs, sn, slots)
        dkv = exchange_back(dkv, ctx, group)
        *before_qkv, g = qkv_backward(dq, dkv, na, h, g1, gains, w_qkv, cs, sn, before_qkv)
    input_grad = redeal(coords, g.reshape(slots, block, width), ctx, group, F32)
    grad_down, grad_gate, grad_up, grad_out, gn_ffn = before_ffn
    grad_qkv, gn_attn = before_qkv
    if tight:
        g_gate, g_up, g_down = finish_ffn(
            gather_sums(split_ffn(coords, grad_gate, grad_up, grad_down))
        )
        g_query, g_key, g_value, g_out, gn_attn, gn_ffn = finish_attn(
            gather_sums(split_attn(coords, grad_qkv, grad_out, gn_attn, gn_ffn))
        )
        gn = (gn_attn[0], gn_ffn[0])
    else:
        gn = lax.psum(jnp.concatenate([gn_attn, gn_ffn], axis=0), "dp")
        gn = lax.psum_scatter(gn, "ctx", scatter_dimension=1, tiled=True)
        g_query = scatter_matrix(grad_qkv[:, :WQ])
        g_key = scatter_matrix(grad_qkv[:, WQ : WQ + WK])
        g_value = scatter_matrix(grad_qkv[:, WQ + WK :])
        g_out = scatter_matrix(grad_out)
        g_gate, g_up, g_down = [scatter_matrix(x) for x in (grad_gate, grad_up, grad_down)]
    return (
        block_output[:, None],
        input_grad[:, None],
        gn[0],
        g_query,
        g_key,
        g_value,
        g_out,
        gn[1],
        g_gate,
        g_up,
        g_down,
    )


def solution(mesh):
    act = P(None, "dp", "ctx", None)
    mat = P("dp", "ctx")
    in_specs = (act, P(None, "dp"), P("ctx"), mat, mat, mat, mat, P("ctx"), mat, mat, mat, act)
    out_specs = (act, act, P("ctx"), mat, mat, mat, mat, P("ctx"), mat, mat, mat)
    return jax.shard_map(body, mesh=mesh, in_specs=in_specs, out_specs=out_specs, check_vma=False)
```

```python
import math

import jax
import jax.numpy as jnp
from jax import lax
from jax.experimental import pallas as pl
from jax.experimental.pallas import tpu as pltpu
from jax.sharding import PartitionSpec as P


H = 9
KV = 3
HD = 64
GRP = H // KV
EPSILON = 1e-05
NEGATIVE = -1e30
BF = jnp.bfloat16
F32 = jnp.float32
VMEM_LIMIT = 56 * 1024 * 1024
SMEM_SPEC = pl.BlockSpec(memory_space=pltpu.SMEM)


def dot(a, b, ca=1, cb=0):
    return lax.dot_general(a, b, (((ca,), (cb,)), ((), ())), preferred_element_type=F32)


def call(body, grid, in_specs, out_specs, out_shape, scratch=()):
    return pl.pallas_call(
        body,
        grid=grid,
        in_specs=in_specs,
        out_specs=out_specs,
        out_shape=out_shape,
        scratch_shapes=list(scratch),
        compiler_params=pltpu.CompilerParams(
            dimension_semantics=("arbitrary",) * len(grid), vmem_limit_bytes=VMEM_LIMIT
        ),
    )


def whole(shape):
    zeros = (0,) * len(shape)
    return pl.BlockSpec(shape, lambda *_: zeros)


def sds(shape, dtype):
    return jax.ShapeDtypeStruct(shape, dtype)


def norm_rows(h):
    return lax.rsqrt(jnp.mean(h * h, -1, keepdims=True) + EPSILON)


def half_swap(x, lane):
    return jnp.where(lane % HD < HD // 2, pltpu.roll(x, 96, 1), pltpu.roll(x, 32, 1))


def place_rows(coords, piece_refs, target_ref):
    slots = len(piece_refs)
    block = piece_refs[0].shape[1]
    for d in range(slots):
        start = pl.multiple_of(lax.rem(coords[1] - d + slots, slots) * block, block)
        value = piece_refs[d][...].astype(F32).T
        target_ref[pl.ds(start, block), :] = value.astype(target_ref.dtype)


def pick_rows(coords, source_ref, piece_refs):
    slots = len(piece_refs)
    block = piece_refs[0].shape[1]
    for d in range(slots):
        start = pl.multiple_of(lax.rem(coords[1] + d, slots) * block, block)
        value = source_ref[pl.ds(start, block), :].T
        piece_refs[d][...] = value.astype(piece_refs[d].dtype)


def qkv_forward(h, gain, w, cs, sn, coords=None):
    dealt = coords is not None
    pieces = list(h) if dealt else [h]
    width, rows = w.shape[0], cs.shape[0]

    def body(*refs):
        if dealt:
            co, *piece_refs = refs[: 1 + len(pieces)]
            refs = refs[1 + len(pieces) :]
            h_ref = refs[-1]
            place_rows(co, piece_refs, h_ref)
        else:
            h_ref, *refs = refs
        g_ref, w_ref, cs_ref, sn_ref, na_ref, q_ref, kv_ref = refs[:7]
        x = h_ref[...]
        na = (x * norm_rows(x) * g_ref[0:1, :]).astype(BF)
        na_ref[...] = na
        y = dot(na, w_ref[...])
        lane = lax.broadcasted_iota(jnp.int32, (rows, 128), 1)
        low = lane < HD
        cosine = cs_ref[...]
        sine = sn_ref[...]
        turned = []
        for c in range((H + KV) // 2):
            x = y[:, 128 * c : 128 * c + 128]
            turned.append(x * cosine + half_swap(x, lane) * sine)
        for head in range(H):
            x = turned[head // 2] * (HD**-0.5)
            if head % 2:
                x = pltpu.roll(x, 64, 1)
            q_ref[head] = jnp.where(low, x, 0.0).astype(BF)
        base = (H + KV) * HD
        for j in range(KV):
            k = turned[(H + j) // 2]
            if (H + j) % 2:
                k = pltpu.roll(k, 64, 1)
            v = y[:, base + HD * j : base + HD * j + HD]
            kv_ref[j] = jnp.concatenate([k[:, :HD], v], axis=1).astype(BF)

    return call(
        body,
        (1,),
        ([SMEM_SPEC] if dealt else [])
        + [whole(x.shape) for x in pieces + [gain, w, cs, sn]],
        [whole((rows, width)), whole((H, rows, 128)), whole((KV, rows, 128))]
        + ([whole((rows, width))] if dealt else []),
        [sds((rows, width), BF), sds((H, rows, 128), BF), sds((KV, rows, 128), BF)]
        + ([sds((rows, width), F32)] if dealt else []),
    )(*([coords] if dealt else []), *pieces, gain, w, cs, sn)


def key_bounds(slots, parts):
    return [max(parts * (s + 1), parts * slots // 2) for s in range(slots)]


def gather_keys(kv_refs, full_ref, slots, block):
    parts = len(kv_refs)
    for t in range(slots):
        for e in range(parts):
            start = (parts * t + e) * block
            full_ref[start : start + block, :] = kv_refs[e][0, t * block : t * block + block, :]


def attend_forward(q, kv_parts, meta, slots):
    parts = len(kv_parts)
    rows = q.shape[1]
    block = rows // slots
    bounds = key_bounds(slots, parts)

    def body(meta_ref, q_ref, *refs):
        kv_refs = refs[:parts]
        att_ref, linv_ref = refs[parts : parts + 2]
        p_refs = refs[parts + 2 : parts + 2 + slots]
        full_ref, turned_ref = refs[-2:]
        gather_keys(kv_refs, full_ref, slots, block)
        turned_ref[...] = full_ref[...].T
        prefix = meta_ref[0]
        lane = lax.broadcasted_iota(jnp.int32, (block, 128), 1)
        for s in range(slots):
            free = parts * s * block
            top = bounds[s] * block
            q_pos = (parts * s + meta_ref[1]) * block + lax.broadcasted_iota(
                jnp.int32, (block, block), 1
            )
            key_iota = lax.broadcasted_iota(jnp.int32, (block, block), 0)
            biases = []
            for t in range(s, bounds[s] // parts):
                for e in range(parts):
                    k_pos = (parts * t + meta_ref[1 + e]) * block + key_iota
                    biases.append(
                        jnp.where((k_pos <= q_pos) | (k_pos < prefix), 0.0, NEGATIVE)
                    )
            bias = jnp.concatenate(biases, axis=0)
            bias = jnp.concatenate([bias] * GRP, axis=1)
            here = slice(s * block, s * block + block)
            qs = q_ref[:, here, :].reshape(GRP * block, 128)
            masked = dot(full_ref[free:top, :], qs, 1, 1) + bias
            top_score = jnp.max(masked, 0, keepdims=True)
            if free:
                opened = dot(full_ref[:free, :], qs, 1, 1)
                top_score = jnp.maximum(top_score, jnp.max(opened, 0, keepdims=True))
            term = jnp.exp(masked - top_score)
            total = jnp.sum(term, 0, keepdims=True)
            pb = term.astype(BF)
            p_refs[s][0, free:top, :] = pb
            mix = dot(turned_ref[:, free:top], pb)
            if free:
                term = jnp.exp(opened - top_score)
                total = total + jnp.sum(term, 0, keepdims=True)
                pb = term.astype(BF)
                p_refs[s][0, :free, :] = pb
                mix = mix + dot(turned_ref[:, :free], pb)
            inverse = 1.0 / total
            sub = lax.broadcasted_iota(jnp.int32, (128, GRP * block), 0)
            mix = jnp.where(sub == 0, inverse, mix * inverse).T
            outs = [mix[hh * block : hh * block + block, HD:].astype(BF) for hh in range(GRP)]
            linvs = [mix[hh * block : hh * block + block, 0:1] for hh in range(GRP)]
            att_ref[0, s * block : s * block + block, :] = jnp.concatenate(outs, axis=1)
            packed = jnp.where(lane == 0, linvs[0], jnp.where(lane == 1, linvs[1], linvs[2]))
            linv_ref[0, s * block : s * block + block, :] = packed

    def head_block(shape):
        return pl.BlockSpec((1,) + shape, lambda j: (j,) + (0,) * len(shape))

    return call(
        body,
        (KV,),
        [
            pl.BlockSpec(memory_space=pltpu.SMEM),
            pl.BlockSpec((GRP, rows, 128), lambda j: (j, 0, 0)),
        ]
        + [head_block((rows, 128))] * parts,
        [head_block((rows, GRP * HD)), head_block((rows, 128))]
        + [head_block((b * block, GRP * block)) for b in bounds],
        [sds((KV, rows, GRP * HD), BF), sds((KV, rows, 128), F32)]
        + [sds((KV, b * block, GRP * block), BF) for b in bounds],
        [pltpu.VMEM((parts * rows, 128), BF), pltpu.VMEM((128, parts * rows), BF)],
    )(meta, q, *kv_parts)


def attend_backward(q, kv_parts, datt, att, linv, probs, cs, sn, slots, first=0, count=KV):
    parts = len(kv_parts)
    rows = q.shape[1]
    block = rows // slots
    bounds = key_bounds(slots, parts)
    total_keys = parts * rows

    def body(q_ref, datt_ref, att_ref, linv_ref, cs_ref, sn_ref, *refs):
        kv_refs = refs[:parts]
        p_refs = refs[parts : parts + slots]
        dq_ref = refs[parts + slots]
        dkv_refs = refs[parts + slots + 1 : parts + slots + 1 + parts]
        full_ref, turned_ref, acc_ref = refs[-3:]
        gather_keys(kv_refs, full_ref, slots, block)
        keys = full_ref[...]
        turned_ref[...] = keys.T
        key_lane = lax.broadcasted_iota(jnp.int32, keys.shape, 1)
        ones = jnp.where(key_lane < 2, 1.0, 0.0)
        full_ref[...] = jnp.where(key_lane < HD, ones, keys.astype(F32)).astype(BF)
        acc_ref[...] = jnp.zeros_like(acc_ref)
        lane = lax.broadcasted_iota(jnp.int32, (block, 128), 1)
        for s in range(slots):
            top = bounds[s] * block
            here = slice(s * block, s * block + block)
            d_all = datt_ref[0, here, :].astype(F32)
            product = d_all * att_ref[0, here, :].astype(F32)
            plain = []
            shifts = []
            for hh in range(GRP):
                inverse = linv_ref[0, here, hh : hh + 1]
                cols = slice(hh * HD, hh * HD + HD)
                delta = jnp.sum(product[:, cols], -1, keepdims=True) * inverse
                scaled = jnp.concatenate(
                    [jnp.zeros((block, HD), F32), d_all[:, cols] * inverse], axis=1
                )
                coarse = delta.astype(BF).astype(F32)
                fine = jnp.where(lane == 1, coarse - delta, 0.0)
                plain.append(scaled.astype(BF))
                shifts.append((scaled + jnp.where(lane == 0, -coarse, fine)).astype(BF))
            plain = jnp.concatenate(plain, axis=0)
            shifts = jnp.concatenate(shifts, axis=0)
            dp = dot(full_ref[:top, :], shifts, 1, 1)
            pb = p_refs[s][0]
            ds = (pb.astype(F32) * dp).astype(BF)
            dq = dot(turned_ref[:, :top], ds).T
            dqs = [dq[hh * block : hh * block + block] for hh in range(GRP)]
            qs = q_ref[:, here, :].reshape(GRP * block, 128)
            acc_ref[:top, :] += dot(
                jnp.concatenate([ds, pb], axis=1), jnp.concatenate([qs, plain], axis=0)
            )
            cosine = cs_ref[here, :]
            sine = sn_ref[here, :]
            outs = []
            for x in dqs:
                x = x * (HD**-0.5)
                x = x * cosine - half_swap(x, lane) * sine
                outs.append(x[:, :HD].astype(BF))
            dq_ref[0, here, :] = jnp.concatenate(outs, axis=1)
        for t in range(slots):
            for e in range(parts):
                start = (parts * t + e) * block
                dkv_refs[e][0, t * block : t * block + block, :] = acc_ref[
                    start : start + block, :
                ].astype(BF)

    def head_block(shape, start=first):
        return pl.BlockSpec((1,) + shape, lambda j: (j + start,) + (0,) * len(shape))

    return call(
        body,
        (count,),
        [
            pl.BlockSpec((GRP, rows, 128), lambda j: (j + first, 0, 0)),
            head_block((rows, GRP * HD)),
            head_block((rows, GRP * HD)),
            head_block((rows, 128)),
            whole(cs.shape),
            whole(sn.shape),
        ]
        + [head_block((rows, 128))] * parts
        + [head_block((b * block, GRP * block)) for b in bounds],
        [head_block((rows, GRP * HD), 0)] + [head_block((rows, 128), 0)] * parts,
        [sds((count, rows, GRP * HD), BF)] + [sds((count, rows, 128), BF)] * parts,
        [
            pltpu.VMEM((total_keys, 128), BF),
            pltpu.VMEM((128, total_keys), BF),
            pltpu.VMEM((total_keys, 128), F32),
        ],
    )(q, datt, att, linv, cs, sn, *kv_parts, *probs)


def ffn_forward(h, att, w_out, gain, w_gate, w_up, w_down, coords=None, slots=4, width_f=512):
    rows, width = h.shape
    ff = w_gate.shape[1]
    steps = ff // width_f
    last = coords is not None

    def body(*refs):
        if last:
            co, *refs = refs
        h_ref, att_ref, wo_ref, g_ref, wg_ref, wu_ref, wd_ref = refs[:7]
        refs = refs[7:]
        h1_ref, nb_ref, a_ref, b_ref, hid_ref, h2_ref = refs[:6]
        f = pl.program_id(0)

        @pl.when(f == 0)
        def _():
            h1 = h_ref[...].astype(F32)
            for j in range(KV):
                h1 = h1 + dot(att_ref[j], wo_ref[GRP * HD * j : GRP * HD * (j + 1), :])
            h1_ref[...] = h1
            h2_ref[...] = h1
            nb_ref[...] = (h1 * norm_rows(h1) * g_ref[1:2, :]).astype(BF)

        nb = nb_ref[...]
        gate = dot(nb, wg_ref[...])
        up = dot(nb, wu_ref[...])
        sig = 1.0 / (1.0 + jnp.exp(-gate))
        silu = gate * sig
        hid = (silu * up).astype(BF)
        hid_ref[...] = hid
        b_ref[...] = silu.astype(BF)
        a_ref[...] = (up * (sig + silu * (1.0 - sig))).astype(BF)
        h2_ref[...] += dot(hid, wd_ref[...], 1, 1)
        if last:

            @pl.when(f == steps - 1)
            def _():
                pick_rows(co, h2_ref, refs[6:])

    tall = pl.BlockSpec((width, width_f), lambda f: (0, f))
    acts = pl.BlockSpec((rows, width_f), lambda f: (0, f))
    out_specs = [whole((rows, width)), whole((rows, width)), acts, acts, acts, whole((rows, width))]
    out_shape = [
        sds((rows, width), F32),
        sds((rows, width), BF),
        sds((rows, ff), BF),
        sds((rows, ff), BF),
        sds((rows, ff), BF),
        sds((rows, width), F32),
    ]
    if last:
        out_specs += [whole((width, rows // slots))] * slots
        out_shape += [sds((width, rows // slots), BF)] * slots
    return call(
        body,
        (steps,),
        ([SMEM_SPEC] if last else [])
        + [
            whole(h.shape),
            whole(att.shape),
            whole(w_out.shape),
            whole(gain.shape),
            tall,
            tall,
            tall,
        ],
        out_specs,
        out_shape,
    )(*([coords] if last else []), h, att, w_out, gain, w_gate, w_up, w_down)


def ffn_backward(g, kept, full, previous, coords=None, width_f=512):
    h1, nb, a, b, hid, att = kept
    w_out, gain, w_gate, w_up, w_down = full
    rows, width = h1.shape
    ff = w_gate.shape[1]
    steps = ff // width_f
    final = previous is not None
    kind = BF if final else F32
    dealt = coords is not None
    streams = list(g) if dealt else [g]

    def body(*refs):
        if dealt:
            co, *refs = refs
        g_refs, refs = refs[: len(streams)], refs[len(streams) - 1 :]
        a_ref, b_ref, hid_ref, nb_ref, h1_ref, att_ref = refs[1:7]
        gain_ref, wo_ref, wg_ref, wu_ref, wd_ref = refs[7:12]
        refs = refs[12:]
        if final:
            pd_ref, pg_ref, pu_ref, po_ref, pn_ref = refs[:5]
            refs = refs[5:]
        gd_ref, gg_ref, gu_ref, go_ref, gn_ref, g1_ref, datt_ref = refs[:7]
        nbt_ref, e2_ref, e2t_ref, dnb_ref = refs[7:]
        f = pl.program_id(0)

        @pl.when(f == 0)
        def _():
            nbt_ref[...] = nb_ref[...].T
            if dealt:
                place_rows(co, g_refs, e2_ref)
            else:
                e2_ref[...] = g_refs[0][...].astype(BF)
            e2t_ref[...] = e2_ref[...].T
            dnb_ref[...] = jnp.zeros_like(dnb_ref)

        e2 = e2_ref[...]
        dh = dot(e2, wd_ref[...])
        dgate = (dh * a_ref[...].astype(F32)).astype(BF)
        dup = (dh * b_ref[...].astype(F32)).astype(BF)
        dnb_ref[...] += dot(dgate, wg_ref[...], 1, 1) + dot(dup, wu_ref[...], 1, 1)
        nbt = nbt_ref[...]
        gd = dot(e2t_ref[...], hid_ref[...])
        gg = dot(nbt, dgate)
        gu = dot(nbt, dup)
        if final:
            gd = gd + pd_ref[...]
            gg = gg + pg_ref[...]
            gu = gu + pu_ref[...]
        gd_ref[...] = gd.astype(kind)
        gg_ref[...] = gg.astype(kind)
        gu_ref[...] = gu.astype(kind)

        @pl.when(f == steps - 1)
        def _():
            h1v = h1_ref[...]
            r = norm_rows(h1v)
            dnb = dnb_ref[...]
            gn = jnp.sum(dnb * h1v * r, 0, keepdims=True)
            u = dnb * gain_ref[1:2, :]
            g1 = (
                (e2_ref if dealt else g_refs[0])[...].astype(F32)
                + r * u
                - h1v * (r * r * r * jnp.mean(u * h1v, -1, keepdims=True))
            )
            g1_ref[...] = g1
            e1 = g1.astype(BF)
            for j in range(KV):
                span = slice(GRP * HD * j, GRP * HD * (j + 1))
                datt_ref[j] = dot(e1, wo_ref[span, :], 1, 1).astype(BF)
                go = dot(att_ref[j], e1, 0, 0)
                if final:
                    go = go + po_ref[span, :]
                go_ref[span, :] = go.astype(kind)
            if final:
                gn = gn + pn_ref[...]
            gn_ref[...] = gn

    tall = pl.BlockSpec((width, width_f), lambda f: (0, f))
    acts = pl.BlockSpec((rows, width_f), lambda f: (0, f))
    one = whole((1, width))
    grads = [tall, tall, tall, whole((width, width)), one]
    return call(
        body,
        (steps,),
        ([SMEM_SPEC] if dealt else [])
        + [whole(x.shape) for x in streams]
        + [acts, acts, acts, whole(nb.shape), whole(h1.shape), whole(att.shape)]
        + [whole(gain.shape), whole(w_out.shape), tall, tall, tall]
        + (grads if final else []),
        grads + [whole((rows, width)), whole((KV, rows, GRP * HD))],
        [
            sds((width, ff), kind),
            sds((width, ff), kind),
            sds((width, ff), kind),
            sds((width, width), kind),
            sds((1, width), F32),
            sds((rows, width), F32),
            sds((KV, rows, GRP * HD), BF),
        ],
        [
            pltpu.VMEM((width, rows), BF),
            pltpu.VMEM((rows, width), BF),
            pltpu.VMEM((width, rows), BF),
            pltpu.VMEM((rows, width), F32),
        ],
    )(
        *([coords] if dealt else []),
        *streams,
        *(a, b, hid, nb, h1, att, gain, w_out, w_gate, w_up, w_down),
        *(previous or ()),
    )


def qkv_backward(dq, dkv, na, h, g1, gain, w, cs, sn, before, coords=None, slots=4):
    rows, width = na.shape
    pieces = len(dq)
    cols = w.shape[1]
    final = coords is not None

    def body(*refs):
        if final:
            co, *refs = refs
        dq_refs, refs = refs[:pieces], refs[pieces:]
        dkv_refs, refs = refs[: len(dkv)], refs[len(dkv) :]
        na_ref, h_ref, g1_ref, gain_ref, w_ref, cs_ref, sn_ref = refs[:7]
        refs = refs[7:]
        if final:
            pn_ref, d_ref, gn_ref, *piece_refs, g0_ref = refs
        else:
            gw_ref, gn_ref, g0_ref = refs
        lane = lax.broadcasted_iota(jnp.int32, (rows, 128), 1)
        cosine = cs_ref[...]
        sine = sn_ref[...]
        ks = []
        vs = []
        for j in range(KV):
            where = [(n, k) for n in range(pieces) for k in range(dq[n].shape[0])][j]
            mine = dkv_refs[where[0] :: pieces]
            x = mine[0][where[1]].astype(F32)
            for ref in mine[1:]:
                x = x + ref[where[1]].astype(F32)
            k = x * cosine - half_swap(x, lane) * sine
            ks.append(k[:, :HD].astype(BF))
            vs.append(x[:, HD:].astype(BF))
        qs = [ref[k] for ref in dq_refs for k in range(ref.shape[0])]
        d = jnp.concatenate(qs + ks + vs, axis=1)
        dna = dot(d, w_ref[...], 1, 1)
        if final:
            d_ref[...] = d
        else:
            gw_ref[...] = dot(na_ref[...], d, 0, 0)
        x = h_ref[...].astype(F32)
        r = norm_rows(x)
        gn = jnp.sum(dna * x * r, 0, keepdims=True)
        u = dna * gain_ref[0:1, :]
        g0_ref[...] = (
            g1_ref[...] + r * u - x * (r * r * r * jnp.mean(u * x, -1, keepdims=True))
        )
        if final:
            gn = gn + pn_ref[...]
            pick_rows(co, g0_ref, piece_refs)
        gn_ref[...] = gn

    args = [*dq, *dkv, na, h, g1, gain, w, cs, sn] + ([before] if final else [])
    shapes = [((1, width), F32)]
    if final:
        shapes = [((rows, cols), BF)] + shapes + [((width, rows // slots), BF)] * slots
    else:
        shapes = [((width, cols), F32)] + shapes + [((rows, width), F32)]
    return call(
        body,
        (1,),
        ([SMEM_SPEC] if final else []) + [whole(x.shape) for x in args],
        [whole(x) for x, _ in shapes],
        [sds(x, t) for x, t in shapes],
        [pltpu.VMEM((rows, width), F32)] if final else [],
    )(*([coords] if final else []), *args)


def qkv_weights(d, na, before):
    def body(d_ref, na_ref, pw_ref, gw_ref):
        gw_ref[...] = (dot(na_ref[...], d_ref[...], 0, 0) + pw_ref[...]).astype(BF)

    args = (d, na, before)
    return call(
        body, (1,), [whole(x.shape) for x in args], [whole(before.shape)], [sds(before.shape, BF)]
    )(*args)[0]


def shifted(total, group, step):
    pairs = []
    for i in range(total):
        z, c = divmod(i, group)
        pairs.append((i, ((z + step) % (total // group)) * group + c))
    return pairs


def within(total, group, step):
    return [(i, (i // group) * group + (i % group + step) % group) for i in range(total)]


WQ = H * HD
WK = KV * HD
COLS_A = (0, 72, 96, 120)
FOLDS = ((0, 32), (32, 32), (64, 32), (96, 32), (128, 16))
ROWS_D = 144
ROWS_F = 256
TOP = ROWS_D


def fold_out(out, cols):
    parts = []
    for start, count in FOLDS:
        part = out[start : start + count, cols]
        if count < 32:
            part = jnp.concatenate([part, jnp.zeros((32 - count, 72), part.dtype)], axis=0)
        parts.append(part)
    return jnp.concatenate(parts + [jnp.zeros((32, 24), out.dtype)], axis=1)


def pack_shards(shards):
    def body(wq, wk, wv, wo, wg, wu, wd, ga, gf, a_ref, top_ref, low_ref):
        wk_rows, wv_rows = [ref[...].astype(F32).T.astype(BF) for ref in (wk, wv)]
        a_ref[:ROWS_D, :] = jnp.concatenate(
            [wq[...], wk_rows, wv_rows, jnp.zeros((ROWS_D, 8), BF)], axis=1
        )
        row = lax.broadcasted_iota(jnp.int32, (16, 72), 0)
        ga_row = ga[...].astype(F32)
        gf_row = gf[...].astype(F32)
        gains = jnp.where(row == 0, ga_row, jnp.where(row == 1, gf_row, 0.0))
        a_ref[ROWS_D:, :] = jnp.concatenate([gains, jnp.zeros((16, 56), F32)], axis=1).astype(BF)
        wide = jnp.concatenate(
            [wg[:, :128], wu[:, :128], wg[:, 128:], wu[:, 128:]], axis=1
        )
        top_ref[...] = wide
        low_ref[:32, :] = fold_out(wo[...], slice(0, 72))
        down = jnp.concatenate(
            [wd[:, :128], wd[:, 192:320], wd[:, 128:192], wd[:, 320:]], axis=1
        ).astype(F32)
        low_ref[32:, :] = jnp.concatenate([down, jnp.zeros((8, 384), F32)], axis=0).astype(BF)

    return call(
        body,
        (1,),
        [whole(x.shape) for x in shards],
        [whole((160, 128)), whole((TOP, 384)), whole((ROWS_F - TOP, 384))],
        [sds((160, 128), BF), sds((TOP, 384), BF), sds((ROWS_F - TOP, 384), BF)],
    )(*shards)


def cross(step, count):
    return [(i, i ^ step) for i in range(count)]


def spread_z(x):
    return [x] + [lax.ppermute(x, "ctx", shifted(8, 2, d)) for d in (1, 2, 3)]


def spread_attn(pieces, mark):
    stack = jnp.stack(pieces)
    mine = [lax.ppermute(stack, "dp", cross(r, 4)) for r in (1, 2, 3)]
    mine = [stack] + after(mine, mark)
    return mine + [lax.ppermute(m, "ctx", cross(1, 8)) for m in mine]


def spread_ffn(top, low):
    top, low = jnp.stack(top), jnp.stack(low)
    top_x = lax.ppermute(top, "dp", cross(1, 4))
    low_y = lax.ppermute(low, "dp", cross(2, 4))
    top_y = lax.ppermute(top, "dp", cross(2, 4))
    low_x = lax.ppermute(low, "dp", cross(1, 4))
    top_far = lax.ppermute(top_x, "dp", cross(2, 4))
    low_far = lax.ppermute(low_y, "dp", cross(1, 4))
    mine = [top, top_x, top_y, top_far, low, low_x, low_y, low_far]
    return mine + [lax.ppermute(m, "ctx", cross(1, 8)) for m in mine]


def ordered(c, own, sibling):
    return jnp.where(c == 0, own, sibling), jnp.where(c == 0, sibling, own)


def assemble_attn(coords, arrays):
    def body(co, *refs):
        own, sib = refs[:4], refs[4:8]
        w_ref, g_ref = refs[8:]
        j_own, z_own, c_own = co[0], co[1], co[2]
        for r in range(4):
            row = pl.multiple_of((j_own ^ r) * ROWS_D, 16)
            pieces = []
            for z in range(4):
                d = lax.rem(z_own - z + 4, 4)
                pieces.extend(ordered(c_own, own[r][d], sib[r][d]))
            groups = [
                jnp.concatenate([p[:ROWS_D, a:b] for p in pieces], axis=1)
                for a, b in zip(COLS_A[:-1], COLS_A[1:])
            ]
            w_ref[pl.ds(row, ROWS_D), :] = jnp.concatenate(groups, axis=1)
            if r == 0:
                g_ref[...] = jnp.concatenate(
                    [p[ROWS_D:, :72].astype(F32) for p in pieces], axis=1
                )

    shapes = [((576, 960), BF), ((16, 576), F32)]
    return call(
        body,
        (1,),
        [SMEM_SPEC] + [whole(x.shape) for x in arrays],
        [whole(s) for s, _ in shapes],
        [sds(s, t) for s, t in shapes],
    )(coords, *arrays)


def assemble_ffn(coords, arrays):
    def body(co, *refs):
        own, sib = refs[:8], refs[8:16]
        o_ref, g_ref, u_ref, d_ref = refs[16:]
        j_own, z_own, c_own = co[0], co[1], co[2]

        def read(group, r, d):
            return jnp.concatenate([group[r][d], group[4 + r][d]], axis=0)

        for r in range(4):
            j = j_own ^ r
            row = pl.multiple_of(j * ROWS_D, 16)
            lane = pl.multiple_of(j * 384, 128)
            pieces = []
            for z in range(4):
                d = lax.rem(z_own - z + 4, 4)
                even, odd = ordered(c_own, read(own, r, d), read(sib, r, d))
                pieces.extend((even, odd))
                here = slice(384 * z, 384 * z + 384)
                for ref, first, rest in ((g_ref, 0, 256), (u_ref, 128, 320)):
                    ref[pl.ds(row, ROWS_D), here] = jnp.concatenate(
                        [
                            even[:ROWS_D, first : first + 128],
                            odd[:ROWS_D, first : first + 128],
                            even[:ROWS_D, rest : rest + 64],
                            odd[:ROWS_D, rest : rest + 64],
                        ],
                        axis=1,
                    )
                down = jnp.concatenate(
                    [even[176:248].astype(F32), odd[176:248].astype(F32)], axis=0
                )
                d_ref[ROWS_D * z : ROWS_D * z + ROWS_D, pl.ds(lane, 384)] = down.astype(BF)
            for g, (start, count) in enumerate(FOLDS):
                o_ref[pl.ds(pl.multiple_of(row + start, 16), count), :] = jnp.concatenate(
                    [p[144 : 144 + count, 72 * g : 72 * g + 72] for p in pieces], axis=1
                )

    shapes = [(576, 576), (576, 1536), (576, 1536), (576, 1536)]
    return call(
        body,
        (1,),
        [SMEM_SPEC] + [whole(x.shape) for x in arrays],
        [whole(s) for s in shapes],
        [sds(s, BF) for s in shapes],
    )(coords, *arrays)


def split_attn(coords, d_qkv, na, before, gn_attn, gn_ffn):
    def body(co, d_ref, na_ref, pw_ref, ga, gf, *outs):
        keep, away, gw = outs[:4], outs[4], outs[5]
        gw[...] = (dot(na_ref[...], d_ref[...], 0, 0) + pw_ref[...]).astype(BF)
        j_own, z_own, c_own = co[0], co[1], co[2]
        sub = lax.broadcasted_iota(jnp.int32, (16, 576), 0)
        gains = jnp.where(sub == 0, ga[...], jnp.where(sub == 1, gf[...], 0.0)).astype(BF)
        for r in range(4):
            row = pl.multiple_of((j_own ^ r) * ROWS_D, 16)
            wide = gw[pl.ds(row, ROWS_D), :]
            for z in range(4):
                d = lax.rem(z - z_own + 4, 4)
                pair = []
                for k in (2 * z, 2 * z + 1):
                    top = jnp.concatenate(
                        [
                            wide[:, 72 * k : 72 * k + 72],
                            wide[:, WQ + 24 * k : WQ + 24 * k + 24],
                            wide[:, WQ + WK + 24 * k : WQ + WK + 24 * k + 24],
                            jnp.zeros((ROWS_D, 8), BF),
                        ],
                        axis=1,
                    )
                    low = jnp.concatenate(
                        [gains[:, 72 * k : 72 * k + 72], jnp.zeros((16, 56), BF)], axis=1
                    )
                    pair.append(jnp.concatenate([top, low], axis=0))
                mine, other = ordered(c_own, *pair)
                keep[r][d] = mine
                away[r, d] = other

    shapes = [(4, 160, 128)] * 4 + [(4, 4, 160, 128)]
    args = (d_qkv, na, before, gn_attn, gn_ffn)
    return call(
        body,
        (1,),
        [SMEM_SPEC] + [whole(x.shape) for x in args],
        [whole(s) for s in shapes],
        [sds(s, BF) for s in shapes],
        [pltpu.VMEM(before.shape, BF)],
    )(coords, *args)


def split_ffn(coords, g_out, g_gate, g_up, g_down):
    def body(co, go, gg, gu, gd, *outs):
        keep, away = outs[:4], outs[4]
        j_own, z_own, c_own = co[0], co[1], co[2]
        for r in range(4):
            j = j_own ^ r
            row = pl.multiple_of(j * ROWS_D, 16)
            lane = pl.multiple_of(j * 384, 128)
            out = go[pl.ds(row, ROWS_D), :]
            for z in range(4):
                d = lax.rem(z - z_own + 4, 4)
                gate = gg[pl.ds(row, ROWS_D), 384 * z : 384 * z + 384]
                up = gu[pl.ds(row, ROWS_D), 384 * z : 384 * z + 384]
                down = gd[ROWS_D * z : ROWS_D * z + ROWS_D, pl.ds(lane, 384)].astype(F32)
                pair = []
                for i in range(2):
                    k = 2 * z + i
                    first = slice(128 * i, 128 * i + 128)
                    rest = slice(256 + 64 * i, 320 + 64 * i)
                    wide = jnp.concatenate(
                        [gate[:, first], up[:, first], gate[:, rest], up[:, rest]], axis=1
                    )
                    low = jnp.concatenate(
                        [down[72 * i : 72 * i + 72], jnp.zeros((8, 384), F32)], axis=0
                    ).astype(BF)
                    pair.append((wide, fold_out(out, slice(72 * k, 72 * k + 72)), low))
                spans = (slice(0, 144), slice(144, 176), slice(176, 256))
                for part, here in enumerate(spans):
                    mine, other = ordered(c_own, pair[0][part], pair[1][part])
                    keep[r][d, here, :] = mine
                    away[r, d, here, :] = other

    shapes = [(4, ROWS_F, 384)] * 4 + [(4, 4, ROWS_F, 384)]
    args = (g_out, g_gate, g_up, g_down)
    return call(
        body,
        (1,),
        [SMEM_SPEC] + [whole(x.shape) for x in args],
        [whole(s) for s in shapes],
        [sds(s, BF) for s in shapes],
    )(coords, *args)


def total(*terms):
    out = terms[0].astype(F32)
    for t in terms[1:]:
        out = out + t.astype(F32)
    return out.astype(BF)


def sum_z(mine):
    return [mine[0]] + [lax.ppermute(mine[d], "ctx", shifted(8, 2, d)) for d in (1, 2, 3)]


def sum_attn(pieces):
    keep, away = pieces[:4], pieces[4]
    back = lax.ppermute(away, "ctx", cross(1, 8))
    moved = [lax.ppermute(total(keep[r], back[r]), "dp", cross(r, 4)) for r in (1, 2, 3)]
    return sum_z(total(keep[0], back[0], *moved))


def sum_ffn(pieces):
    keep, away = pieces[:4], pieces[4]
    back = lax.ppermute(away, "ctx", cross(1, 8))
    top, low = slice(0, TOP), slice(TOP, ROWS_F)

    def pair(r, rows, *more):
        return total(keep[r][:, rows], back[r][:, rows], *more)

    far_top, far_low = pair(3, top), pair(3, low)
    x_low, y_top = pair(1, low), pair(2, top)
    top_far = lax.ppermute(far_top, "dp", cross(2, 4))
    low_far = lax.ppermute(far_low, "dp", cross(1, 4))
    low_x = lax.ppermute(x_low, "dp", cross(1, 4))
    top_y = lax.ppermute(y_top, "dp", cross(2, 4))
    x_top, y_low = pair(1, top, top_far), pair(2, low, low_far)
    top_x = lax.ppermute(x_top, "dp", cross(1, 4))
    low_y = lax.ppermute(y_low, "dp", cross(2, 4))
    mine = jnp.concatenate([pair(0, top, top_x, top_y), pair(0, low, low_x, low_y)], axis=1)
    return sum_z(mine), (away, (far_top, far_low, x_low, y_top))


def finish(terms_f, terms_a):
    def body(*refs):
        o_ref, g_ref, u_ref, d_ref, q_ref, k_ref, v_ref, ga_ref, gf_ref = refs[8:]
        x = sum(ref[...].astype(F32) for ref in refs[4:8])
        q_ref[...] = x[:ROWS_D, :72]
        k_ref[...] = x[:ROWS_D, 72:96].T
        v_ref[...] = x[:ROWS_D, 96:120].T
        ga_ref[...] = x[ROWS_D : ROWS_D + 1, :72]
        gf_ref[...] = x[ROWS_D + 1 : ROWS_D + 2, :72]
        x = sum(ref[...].astype(F32) for ref in refs[:4])
        wide = x[:ROWS_D]
        g_ref[...] = jnp.concatenate([wide[:, :128], wide[:, 256:320]], axis=1)
        u_ref[...] = jnp.concatenate([wide[:, 128:256], wide[:, 320:]], axis=1)
        for g, (start, count) in enumerate(FOLDS):
            o_ref[start : start + count, :] = x[144 : 144 + count, 72 * g : 72 * g + 72]
        low = x[176:248]
        d_ref[...] = jnp.concatenate(
            [low[:, :128], low[:, 256:320], low[:, 128:256], low[:, 320:]], axis=1
        )

    shapes = [(ROWS_D, 72), (ROWS_D, 192), (ROWS_D, 192), (72, 384)]
    shapes += [(ROWS_D, 72), (24, ROWS_D), (24, ROWS_D), (1, 72), (1, 72)]
    terms = [*terms_f, *terms_a]
    return call(
        body,
        (1,),
        [whole(x.shape) for x in terms],
        [whole(s) for s in shapes],
        [sds(s, F32) for s in shapes],
    )(*terms)


def pick_slots(coords, x):
    slots, width, rows = x.shape

    def body(co, x_ref, *outs):
        for d in range(slots):
            outs[d][...] = x_ref[lax.rem(co[1] + d, slots)]

    return call(
        body,
        (1,),
        [SMEM_SPEC, whole(x.shape)],
        [whole((width, rows))] * slots,
        [sds((width, rows), BF)] * slots,
    )(coords, x)


def place_slots(coords, pieces, dtype):
    slots = len(pieces)
    width, rows = pieces[0].shape

    def body(co, *refs):
        for d in range(slots):
            refs[slots][lax.rem(co[1] - d + slots, slots)] = refs[d][...].astype(dtype)

    return call(
        body,
        (1,),
        [SMEM_SPEC] + [whole((width, rows))] * slots,
        [whole((slots, width, rows))],
        [sds((slots, width, rows), dtype)],
    )(coords, *pieces)[0]


def redeal(pieces, ctx, group):
    return [pieces[0]] + [
        lax.ppermute(pieces[d], "ctx", shifted(ctx, group, d))
        for d in range(1, len(pieces))
    ]


def exchange(kv, ctx, group):
    return [kv] + [lax.ppermute(kv, "ctx", within(ctx, group, e)) for e in range(1, group)]


def after(x, mark):
    return lax.optimization_barrier((x, mark))[0]


def tables(slots, block, group):
    c = lax.axis_index("ctx") % group
    half_width = HD // 2
    frequency = jnp.exp(jnp.arange(half_width, dtype=F32) * (-2.0 * math.log(10000.0) / HD))
    positions = (group * jnp.arange(slots)[:, None] + c) * block + jnp.arange(block)[None, :]
    angles = positions.reshape(-1).astype(F32)[:, None] * frequency[None, :]
    cosine, sine = jnp.cos(angles), jnp.sin(angles)
    return (
        jnp.concatenate([cosine] * 4, axis=1),
        jnp.concatenate([-sine, sine, -sine, sine], axis=1),
    )


def gather_matrix(shard):
    return lax.all_gather(
        lax.all_gather(shard, "ctx", axis=1, tiled=True), "dp", axis=0, tiled=True
    )


def scatter_matrix(grad):
    part = lax.psum_scatter(grad, "dp", scatter_dimension=0, tiled=True)
    return lax.psum_scatter(part, "ctx", scatter_dimension=1, tiled=True).astype(F32)


def step(
    tokens,
    prefix,
    norm_attn,
    w_query,
    w_key,
    w_value,
    w_output,
    norm_ffn,
    w_gate,
    w_up,
    w_down,
    cotangent,
):
    slots, _, block, width = tokens.shape
    ctx = lax.axis_size("ctx")
    group = ctx // slots
    index = lax.axis_index("ctx")
    c = index % group
    cs, sn = tables(slots, block, group)
    micro_prefix = lax.dynamic_index_in_dim(prefix[:, 0], index // group, 0, keepdims=True)
    members = (c - jnp.arange(group)) % group
    meta = jnp.concatenate([micro_prefix, members]).astype(jnp.int32)

    dp = lax.axis_size("dp")
    coords = jnp.stack([lax.axis_index("dp"), index // group, c]).astype(jnp.int32)
    tight = dp == 4 and ctx == 8 and slots == 4 and w_query.shape == (ROWS_D, 72)

    own_tokens = jnp.swapaxes(tokens[:, 0], 1, 2)
    if tight:
        shards = (w_query, w_key.T, w_value.T, w_output, w_gate, w_up, w_down.T)
        pack_a, pack_top, pack_low = pack_shards(shards + (norm_attn[None], norm_ffn[None]))
        stack_a = spread_z(pack_a)
        picked = pick_slots(coords, after(own_tokens, pack_a))
        h = redeal(picked, ctx, group)
        w_qkv, gains = assemble_attn(coords, spread_attn(stack_a, (cs, sn, meta)))
        spread = spread_ffn(spread_z(pack_top), spread_z(pack_low))
        w_out, *w_ffn = assemble_ffn(coords, spread)
    else:
        gains = lax.all_gather(jnp.stack([norm_attn, norm_ffn]), "ctx", axis=1, tiled=True)
        gains = jnp.concatenate([gains.astype(F32), jnp.zeros((14, width), F32)], axis=0)
        w_qkv = jnp.concatenate(
            [gather_matrix(w_query), gather_matrix(w_key), gather_matrix(w_value)], axis=1
        )
        h = redeal(pick_slots(coords, own_tokens), ctx, group)
        w_out = gather_matrix(w_output)
        w_ffn = [gather_matrix(w_gate), gather_matrix(w_up), gather_matrix(w_down).T]
    full = (w_out, gains, *w_ffn)

    kept = []
    for layer in range(2):
        last = layer == 1
        na, q, kv, *dealt = qkv_forward(h, gains, w_qkv, cs, sn, None if last else coords)
        if dealt:
            h = dealt[0]
        kv_parts = exchange(kv, ctx, group)
        att, linv, *probs = attend_forward(q, kv_parts, meta, slots)
        h1, nb, a, b, hid, h2, *out_pieces = ffn_forward(
            h, att, *full, coords if last else None, slots
        )
        kept.append((h, na, q, kv_parts, att, linv, probs, h1, nb, a, b, hid))
        h = h2

    g = pick_slots(coords, jnp.swapaxes(cotangent[:, 0], 1, 2))
    g = redeal(g, ctx, group)
    out_pieces = redeal(out_pieces, ctx, group)
    block_output = place_slots(coords, out_pieces, BF)
    before_ffn = None
    for layer in (1, 0):
        h, na, q, kv_parts, att, linv, probs, h1, nb, a, b, hid = kept[layer]
        *before_ffn, g1, datt = ffn_backward(
            g, (h1, nb, a, b, hid, att), full, before_ffn, coords if layer == 1 else None
        )
        back_args = (q, kv_parts, datt, att, linv, probs, cs, sn, slots)
        chunks = [(0, KV)] if layer == 1 else [(0, 1), (1, KV - 1)]
        if layer == 0 and tight:
            grad_down, grad_gate, grad_up, grad_out, gn_ffn = before_ffn
            parts_f = split_ffn(coords, grad_out, grad_gate, grad_up, grad_down)
            terms_f, marks = sum_ffn(parts_f)
        dq, sent = [], []
        for n, (first, count) in enumerate(chunks):
            args = back_args
            if layer == 0 and tight:
                args = (after(q, marks[n]),) + back_args[1:]
            got = attend_backward(*args, first, count)
            dq.append(got[0])
            sent.append(got[1:])
        own = [parts[0] for parts in sent]
        moved = [
            lax.ppermute(parts[e], "ctx", within(ctx, group, -e))
            for e in range(1, group)
            for parts in sent
        ]
        dkv = own + moved
        back = (dq, dkv, na, h, g1, gains, w_qkv, cs, sn)
        if layer == 1:
            before_qkv, gn_attn, g = qkv_backward(*back, None)
        else:
            d_qkv, gn_attn, *g = qkv_backward(*back, gn_attn, coords, slots)
    input_grad = place_slots(coords, redeal(g, ctx, group), F32)
    grad_down, grad_gate, grad_up, grad_out, gn_ffn = before_ffn
    if tight:
        split = split_attn(coords, d_qkv, na, before_qkv, gn_attn, gn_ffn)
        done = finish(terms_f, sum_attn(split))
        g_out, g_gate, g_up, g_down, g_query, g_key, g_value, gn_attn, gn_ffn = done
        g_key, g_value, g_down = g_key.T, g_value.T, g_down.T
        gn = (gn_attn[0], gn_ffn[0])
    else:
        gn = lax.psum(jnp.concatenate([gn_attn, gn_ffn], axis=0), "dp")
        gn = lax.psum_scatter(gn, "ctx", scatter_dimension=1, tiled=True)
        grad_qkv = qkv_weights(d_qkv, na, before_qkv)
        g_query = scatter_matrix(grad_qkv[:, :WQ])
        g_key = scatter_matrix(grad_qkv[:, WQ : WQ + WK])
        g_value = scatter_matrix(grad_qkv[:, WQ + WK :])
        g_out = scatter_matrix(grad_out)
        g_gate, g_up, g_down = [scatter_matrix(x) for x in (grad_gate, grad_up, grad_down.T)]
    return (
        jnp.swapaxes(block_output, 1, 2)[:, None],
        jnp.swapaxes(input_grad, 1, 2)[:, None],
        gn[0],
        g_query,
        g_key,
        g_value,
        g_out,
        gn[1],
        g_gate,
        g_up,
        g_down,
    )


def solution(mesh):
    act = P(None, "dp", "ctx", None)
    mat = P("dp", "ctx")
    in_specs = (act, P(None, "dp"), P("ctx"), mat, mat, mat, mat, P("ctx"), mat, mat, mat, act)
    out_specs = (act, act, P("ctx"), mat, mat, mat, mat, P("ctx"), mat, mat, mat)
    return jax.shard_map(step, mesh=mesh, in_specs=in_specs, out_specs=out_specs, check_vma=False)
```

```python
import math

import jax
import jax.numpy as jnp
from jax import lax
from jax.experimental import pallas as pl
from jax.experimental.pallas import tpu as pltpu
from jax.sharding import PartitionSpec as P


H = 9
KV = 3
HD = 64
GRP = H // KV
EPSILON = 1e-05
NEGATIVE = -1e30
BF = jnp.bfloat16
F32 = jnp.float32
VMEM_LIMIT = 56 * 1024 * 1024
SMEM_SPEC = pl.BlockSpec(memory_space=pltpu.SMEM)


def dot(a, b, ca=1, cb=0):
    return lax.dot_general(a, b, (((ca,), (cb,)), ((), ())), preferred_element_type=F32)


def call(body, grid, in_specs, out_specs, out_shape, scratch=()):
    return pl.pallas_call(
        body,
        grid=grid,
        in_specs=in_specs,
        out_specs=out_specs,
        out_shape=out_shape,
        scratch_shapes=list(scratch),
        compiler_params=pltpu.CompilerParams(
            dimension_semantics=("arbitrary",) * len(grid), vmem_limit_bytes=VMEM_LIMIT
        ),
    )


def whole(shape):
    zeros = (0,) * len(shape)
    return pl.BlockSpec(shape, lambda *_: zeros)


def sds(shape, dtype):
    return jax.ShapeDtypeStruct(shape, dtype)


def norm_rows(h):
    return lax.rsqrt(jnp.mean(h * h, -1, keepdims=True) + EPSILON)


def half_swap(x, lane):
    return jnp.where(lane % HD < HD // 2, pltpu.roll(x, 96, 1), pltpu.roll(x, 32, 1))


def place_rows(coords, piece_refs, target_ref):
    slots = len(piece_refs)
    block = piece_refs[0].shape[1]
    for d in range(slots):
        start = pl.multiple_of(lax.rem(coords[1] - d + slots, slots) * block, block)
        value = piece_refs[d][...].astype(F32).T
        target_ref[pl.ds(start, block), :] = value.astype(target_ref.dtype)


def pick_rows(coords, source_ref, piece_refs):
    slots = len(piece_refs)
    block = piece_refs[0].shape[1]
    for d in range(slots):
        start = pl.multiple_of(lax.rem(coords[1] + d, slots) * block, block)
        value = source_ref[pl.ds(start, block), :].T
        piece_refs[d][...] = value.astype(piece_refs[d].dtype)


def qkv_forward(h, gain, w, cs, sn, coords=None):
    dealt = coords is not None
    pieces = list(h) if dealt else [h]
    width, rows = w.shape[0], cs.shape[0]

    def body(*refs):
        if dealt:
            co, *piece_refs = refs[: 1 + len(pieces)]
            refs = refs[1 + len(pieces) :]
            h_ref = refs[-1]
            place_rows(co, piece_refs, h_ref)
        else:
            h_ref, *refs = refs
        g_ref, w_ref, cs_ref, sn_ref, na_ref, q_ref, kv_ref = refs[:7]
        x = h_ref[...]
        na = (x * norm_rows(x) * g_ref[0:1, :]).astype(BF)
        na_ref[...] = na
        y = dot(na, w_ref[...])
        lane = lax.broadcasted_iota(jnp.int32, (rows, 128), 1)
        low = lane < HD
        cosine = cs_ref[...]
        sine = sn_ref[...]
        turned = []
        for c in range((H + KV) // 2):
            x = y[:, 128 * c : 128 * c + 128]
            turned.append(x * cosine + half_swap(x, lane) * sine)
        for head in range(H):
            x = turned[head // 2] * (HD**-0.5)
            if head % 2:
                x = pltpu.roll(x, 64, 1)
            q_ref[head] = jnp.where(low, x, 0.0).astype(BF)
        base = (H + KV) * HD
        for j in range(KV):
            k = turned[(H + j) // 2]
            if (H + j) % 2:
                k = pltpu.roll(k, 64, 1)
            v = y[:, base + HD * j : base + HD * j + HD]
            kv_ref[j] = jnp.concatenate([k[:, :HD], v], axis=1).astype(BF)

    return call(
        body,
        (1,),
        ([SMEM_SPEC] if dealt else [])
        + [whole(x.shape) for x in pieces + [gain, w, cs, sn]],
        [whole((rows, width)), whole((H, rows, 128)), whole((KV, rows, 128))]
        + ([whole((rows, width))] if dealt else []),
        [sds((rows, width), BF), sds((H, rows, 128), BF), sds((KV, rows, 128), BF)]
        + ([sds((rows, width), F32)] if dealt else []),
    )(*([coords] if dealt else []), *pieces, gain, w, cs, sn)


def key_bounds(slots, parts):
    return [max(parts * (s + 1), parts * slots // 2) for s in range(slots)]


def gather_keys(kv_refs, full_ref, slots, block):
    parts = len(kv_refs)
    for t in range(slots):
        for e in range(parts):
            start = (parts * t + e) * block
            full_ref[start : start + block, :] = kv_refs[e][0, t * block : t * block + block, :]


def attend_forward(q, kv_parts, meta, slots):
    parts = len(kv_parts)
    rows = q.shape[1]
    block = rows // slots
    bounds = key_bounds(slots, parts)

    def body(meta_ref, q_ref, *refs):
        kv_refs = refs[:parts]
        att_ref, linv_ref = refs[parts : parts + 2]
        p_refs = refs[parts + 2 : parts + 2 + slots]
        full_ref, turned_ref = refs[-2:]
        gather_keys(kv_refs, full_ref, slots, block)
        turned_ref[...] = full_ref[...].T
        prefix = meta_ref[0]
        lane = lax.broadcasted_iota(jnp.int32, (block, 128), 1)
        for s in range(slots):
            free = parts * s * block
            top = bounds[s] * block
            q_pos = (parts * s + meta_ref[1]) * block + lax.broadcasted_iota(
                jnp.int32, (block, block), 1
            )
            key_iota = lax.broadcasted_iota(jnp.int32, (block, block), 0)
            biases = []
            for t in range(s, bounds[s] // parts):
                for e in range(parts):
                    k_pos = (parts * t + meta_ref[1 + e]) * block + key_iota
                    biases.append(
                        jnp.where((k_pos <= q_pos) | (k_pos < prefix), 0.0, NEGATIVE)
                    )
            bias = jnp.concatenate(biases, axis=0)
            bias = jnp.concatenate([bias] * GRP, axis=1)
            here = slice(s * block, s * block + block)
            qs = q_ref[:, here, :].reshape(GRP * block, 128)
            masked = dot(full_ref[free:top, :], qs, 1, 1) + bias
            top_score = jnp.max(masked, 0, keepdims=True)
            if free:
                opened = dot(full_ref[:free, :], qs, 1, 1)
                top_score = jnp.maximum(top_score, jnp.max(opened, 0, keepdims=True))
            term = jnp.exp(masked - top_score)
            total = jnp.sum(term, 0, keepdims=True)
            pb = term.astype(BF)
            p_refs[s][0, free:top, :] = pb
            mix = dot(turned_ref[:, free:top], pb)
            if free:
                term = jnp.exp(opened - top_score)
                total = total + jnp.sum(term, 0, keepdims=True)
                pb = term.astype(BF)
                p_refs[s][0, :free, :] = pb
                mix = mix + dot(turned_ref[:, :free], pb)
            inverse = 1.0 / total
            sub = lax.broadcasted_iota(jnp.int32, (128, GRP * block), 0)
            mix = jnp.where(sub == 0, inverse, mix * inverse).T
            outs = [mix[hh * block : hh * block + block, HD:].astype(BF) for hh in range(GRP)]
            linvs = [mix[hh * block : hh * block + block, 0:1] for hh in range(GRP)]
            att_ref[0, s * block : s * block + block, :] = jnp.concatenate(outs, axis=1)
            packed = jnp.where(lane == 0, linvs[0], jnp.where(lane == 1, linvs[1], linvs[2]))
            linv_ref[0, s * block : s * block + block, :] = packed

    def head_block(shape):
        return pl.BlockSpec((1,) + shape, lambda j: (j,) + (0,) * len(shape))

    return call(
        body,
        (KV,),
        [
            pl.BlockSpec(memory_space=pltpu.SMEM),
            pl.BlockSpec((GRP, rows, 128), lambda j: (j, 0, 0)),
        ]
        + [head_block((rows, 128))] * parts,
        [head_block((rows, GRP * HD)), head_block((rows, 128))]
        + [head_block((b * block, GRP * block)) for b in bounds],
        [sds((KV, rows, GRP * HD), BF), sds((KV, rows, 128), F32)]
        + [sds((KV, b * block, GRP * block), BF) for b in bounds],
        [pltpu.VMEM((parts * rows, 128), BF), pltpu.VMEM((128, parts * rows), BF)],
    )(meta, q, *kv_parts)


def attend_backward(q, kv_parts, datt, att, linv, probs, cs, sn, slots, first=0, count=KV):
    parts = len(kv_parts)
    rows = q.shape[1]
    block = rows // slots
    bounds = key_bounds(slots, parts)
    total_keys = parts * rows

    def body(q_ref, datt_ref, att_ref, linv_ref, cs_ref, sn_ref, *refs):
        kv_refs = refs[:parts]
        p_refs = refs[parts : parts + slots]
        dq_ref = refs[parts + slots]
        dkv_refs = refs[parts + slots + 1 : parts + slots + 1 + parts]
        full_ref, turned_ref, acc_ref = refs[-3:]
        gather_keys(kv_refs, full_ref, slots, block)
        keys = full_ref[...]
        turned_ref[...] = keys.T
        key_lane = lax.broadcasted_iota(jnp.int32, keys.shape, 1)
        ones = jnp.where(key_lane < 2, 1.0, 0.0)
        full_ref[...] = jnp.where(key_lane < HD, ones, keys.astype(F32)).astype(BF)
        acc_ref[...] = jnp.zeros_like(acc_ref)
        lane = lax.broadcasted_iota(jnp.int32, (block, 128), 1)
        for s in range(slots):
            top = bounds[s] * block
            here = slice(s * block, s * block + block)
            d_all = datt_ref[0, here, :].astype(F32)
            product = d_all * att_ref[0, here, :].astype(F32)
            plain = []
            shifts = []
            for hh in range(GRP):
                inverse = linv_ref[0, here, hh : hh + 1]
                cols = slice(hh * HD, hh * HD + HD)
                delta = jnp.sum(product[:, cols], -1, keepdims=True) * inverse
                scaled = jnp.concatenate(
                    [jnp.zeros((block, HD), F32), d_all[:, cols] * inverse], axis=1
                )
                coarse = delta.astype(BF).astype(F32)
                fine = jnp.where(lane == 1, coarse - delta, 0.0)
                plain.append(scaled.astype(BF))
                shifts.append((scaled + jnp.where(lane == 0, -coarse, fine)).astype(BF))
            plain = jnp.concatenate(plain, axis=0)
            shifts = jnp.concatenate(shifts, axis=0)
            dp = dot(full_ref[:top, :], shifts, 1, 1)
            pb = p_refs[s][0]
            ds = (pb.astype(F32) * dp).astype(BF)
            dq = dot(turned_ref[:, :top], ds).T
            dqs = [dq[hh * block : hh * block + block] for hh in range(GRP)]
            qs = q_ref[:, here, :].reshape(GRP * block, 128)
            acc_ref[:top, :] += dot(
                jnp.concatenate([ds, pb], axis=1), jnp.concatenate([qs, plain], axis=0)
            )
            cosine = cs_ref[here, :]
            sine = sn_ref[here, :]
            outs = []
            for x in dqs:
                x = x * (HD**-0.5)
                x = x * cosine - half_swap(x, lane) * sine
                outs.append(x[:, :HD].astype(BF))
            dq_ref[0, here, :] = jnp.concatenate(outs, axis=1)
        for t in range(slots):
            for e in range(parts):
                start = (parts * t + e) * block
                dkv_refs[e][0, t * block : t * block + block, :] = acc_ref[
                    start : start + block, :
                ].astype(BF)

    def head_block(shape, start=first):
        return pl.BlockSpec((1,) + shape, lambda j: (j + start,) + (0,) * len(shape))

    return call(
        body,
        (count,),
        [
            pl.BlockSpec((GRP, rows, 128), lambda j: (j + first, 0, 0)),
            head_block((rows, GRP * HD)),
            head_block((rows, GRP * HD)),
            head_block((rows, 128)),
            whole(cs.shape),
            whole(sn.shape),
        ]
        + [head_block((rows, 128))] * parts
        + [head_block((b * block, GRP * block)) for b in bounds],
        [head_block((rows, GRP * HD), 0)] + [head_block((rows, 128), 0)] * parts,
        [sds((count, rows, GRP * HD), BF)] + [sds((count, rows, 128), BF)] * parts,
        [
            pltpu.VMEM((total_keys, 128), BF),
            pltpu.VMEM((128, total_keys), BF),
            pltpu.VMEM((total_keys, 128), F32),
        ],
    )(q, datt, att, linv, cs, sn, *kv_parts, *probs)


def ffn_forward(h, att, w_out, gain, w_gate, w_up, w_down, coords=None, slots=4, width_f=512):
    rows, width = h.shape
    ff = w_gate.shape[1]
    steps = ff // width_f
    last = coords is not None

    def body(*refs):
        if last:
            co, *refs = refs
        h_ref, att_ref, wo_ref, g_ref, wg_ref, wu_ref, wd_ref = refs[:7]
        refs = refs[7:]
        h1_ref, nb_ref, a_ref, b_ref, hid_ref, h2_ref = refs[:6]
        f = pl.program_id(0)

        @pl.when(f == 0)
        def _():
            h1 = h_ref[...].astype(F32)
            for j in range(KV):
                h1 = h1 + dot(att_ref[j], wo_ref[GRP * HD * j : GRP * HD * (j + 1), :])
            h1_ref[...] = h1
            h2_ref[...] = h1
            nb_ref[...] = (h1 * norm_rows(h1) * g_ref[1:2, :]).astype(BF)

        nb = nb_ref[...]
        gate = dot(nb, wg_ref[...])
        up = dot(nb, wu_ref[...])
        sig = 1.0 / (1.0 + jnp.exp(-gate))
        silu = gate * sig
        hid = (silu * up).astype(BF)
        hid_ref[...] = hid
        b_ref[...] = silu.astype(BF)
        a_ref[...] = (up * (sig + silu * (1.0 - sig))).astype(BF)
        h2_ref[...] += dot(hid, wd_ref[...], 1, 1)
        if last:

            @pl.when(f == steps - 1)
            def _():
                pick_rows(co, h2_ref, refs[6:])

    tall = pl.BlockSpec((width, width_f), lambda f: (0, f))
    acts = pl.BlockSpec((rows, width_f), lambda f: (0, f))
    out_specs = [whole((rows, width)), whole((rows, width)), acts, acts, acts, whole((rows, width))]
    out_shape = [
        sds((rows, width), F32),
        sds((rows, width), BF),
        sds((rows, ff), BF),
        sds((rows, ff), BF),
        sds((rows, ff), BF),
        sds((rows, width), F32),
    ]
    if last:
        out_specs += [whole((width, rows // slots))] * slots
        out_shape += [sds((width, rows // slots), BF)] * slots
    return call(
        body,
        (steps,),
        ([SMEM_SPEC] if last else [])
        + [
            whole(h.shape),
            whole(att.shape),
            whole(w_out.shape),
            whole(gain.shape),
            tall,
            tall,
            tall,
        ],
        out_specs,
        out_shape,
    )(*([coords] if last else []), h, att, w_out, gain, w_gate, w_up, w_down)


def ffn_backward(g, kept, full, previous, coords=None, width_f=512):
    h1, nb, a, b, hid, att = kept
    w_out, gain, w_gate, w_up, w_down = full
    rows, width = h1.shape
    ff = w_gate.shape[1]
    steps = ff // width_f
    final = previous is not None
    kind = BF if final else F32
    dealt = coords is not None
    streams = list(g) if dealt else [g]

    def body(*refs):
        if dealt:
            co, *refs = refs
        g_refs, refs = refs[: len(streams)], refs[len(streams) - 1 :]
        a_ref, b_ref, hid_ref, nb_ref, h1_ref, att_ref = refs[1:7]
        gain_ref, wo_ref, wg_ref, wu_ref, wd_ref = refs[7:12]
        refs = refs[12:]
        if final:
            pd_ref, pg_ref, pu_ref, po_ref, pn_ref = refs[:5]
            refs = refs[5:]
        gd_ref, gg_ref, gu_ref, go_ref, gn_ref, g1_ref, datt_ref = refs[:7]
        nbt_ref, e2_ref, e2t_ref, dnb_ref = refs[7:]
        f = pl.program_id(0)

        @pl.when(f == 0)
        def _():
            nbt_ref[...] = nb_ref[...].T
            if dealt:
                place_rows(co, g_refs, e2_ref)
            else:
                e2_ref[...] = g_refs[0][...].astype(BF)
            e2t_ref[...] = e2_ref[...].T
            dnb_ref[...] = jnp.zeros_like(dnb_ref)

        e2 = e2_ref[...]
        dh = dot(e2, wd_ref[...])
        dgate = (dh * a_ref[...].astype(F32)).astype(BF)
        dup = (dh * b_ref[...].astype(F32)).astype(BF)
        dnb_ref[...] += dot(dgate, wg_ref[...], 1, 1) + dot(dup, wu_ref[...], 1, 1)
        nbt = nbt_ref[...]
        gd = dot(e2t_ref[...], hid_ref[...])
        gg = dot(nbt, dgate)
        gu = dot(nbt, dup)
        if final:
            gd = gd + pd_ref[...]
            gg = gg + pg_ref[...]
            gu = gu + pu_ref[...]
        gd_ref[...] = gd.astype(kind)
        gg_ref[...] = gg.astype(kind)
        gu_ref[...] = gu.astype(kind)

        @pl.when(f == steps - 1)
        def _():
            h1v = h1_ref[...]
            r = norm_rows(h1v)
            dnb = dnb_ref[...]
            gn = jnp.sum(dnb * h1v * r, 0, keepdims=True)
            u = dnb * gain_ref[1:2, :]
            g1 = (
                (e2_ref if dealt else g_refs[0])[...].astype(F32)
                + r * u
                - h1v * (r * r * r * jnp.mean(u * h1v, -1, keepdims=True))
            )
            g1_ref[...] = g1
            e1 = g1.astype(BF)
            for j in range(KV):
                span = slice(GRP * HD * j, GRP * HD * (j + 1))
                datt_ref[j] = dot(e1, wo_ref[span, :], 1, 1).astype(BF)
                go = dot(att_ref[j], e1, 0, 0)
                if final:
                    go = go + po_ref[span, :]
                go_ref[span, :] = go.astype(kind)
            if final:
                gn = gn + pn_ref[...]
            gn_ref[...] = gn

    tall = pl.BlockSpec((width, width_f), lambda f: (0, f))
    acts = pl.BlockSpec((rows, width_f), lambda f: (0, f))
    one = whole((1, width))
    grads = [tall, tall, tall, whole((width, width)), one]
    return call(
        body,
        (steps,),
        ([SMEM_SPEC] if dealt else [])
        + [whole(x.shape) for x in streams]
        + [acts, acts, acts, whole(nb.shape), whole(h1.shape), whole(att.shape)]
        + [whole(gain.shape), whole(w_out.shape), tall, tall, tall]
        + (grads if final else []),
        grads + [whole((rows, width)), whole((KV, rows, GRP * HD))],
        [
            sds((width, ff), kind),
            sds((width, ff), kind),
            sds((width, ff), kind),
            sds((width, width), kind),
            sds((1, width), F32),
            sds((rows, width), F32),
            sds((KV, rows, GRP * HD), BF),
        ],
        [
            pltpu.VMEM((width, rows), BF),
            pltpu.VMEM((rows, width), BF),
            pltpu.VMEM((width, rows), BF),
            pltpu.VMEM((rows, width), F32),
        ],
    )(
        *([coords] if dealt else []),
        *streams,
        *(a, b, hid, nb, h1, att, gain, w_out, w_gate, w_up, w_down),
        *(previous or ()),
    )


def qkv_backward(dq, dkv, na, h, g1, gain, w, cs, sn, before, coords=None, slots=4):
    rows, width = na.shape
    pieces = len(dq)
    cols = w.shape[1]
    final = coords is not None

    def body(*refs):
        if final:
            co, *refs = refs
        dq_refs, refs = refs[:pieces], refs[pieces:]
        dkv_refs, refs = refs[: len(dkv)], refs[len(dkv) :]
        na_ref, h_ref, g1_ref, gain_ref, w_ref, cs_ref, sn_ref = refs[:7]
        refs = refs[7:]
        if final:
            pn_ref, d_ref, gn_ref, *piece_refs, g0_ref = refs
        else:
            gw_ref, gn_ref, g0_ref = refs
        lane = lax.broadcasted_iota(jnp.int32, (rows, 128), 1)
        cosine = cs_ref[...]
        sine = sn_ref[...]
        ks = []
        vs = []
        for j in range(KV):
            where = [(n, k) for n in range(pieces) for k in range(dq[n].shape[0])][j]
            mine = dkv_refs[where[0] :: pieces]
            x = mine[0][where[1]].astype(F32)
            for ref in mine[1:]:
                x = x + ref[where[1]].astype(F32)
            k = x * cosine - half_swap(x, lane) * sine
            ks.append(k[:, :HD].astype(BF))
            vs.append(x[:, HD:].astype(BF))
        qs = [ref[k] for ref in dq_refs for k in range(ref.shape[0])]
        d = jnp.concatenate(qs + ks + vs, axis=1)
        dna = dot(d, w_ref[...], 1, 1)
        if final:
            d_ref[...] = d
        else:
            gw_ref[...] = dot(na_ref[...], d, 0, 0)
        x = h_ref[...].astype(F32)
        r = norm_rows(x)
        gn = jnp.sum(dna * x * r, 0, keepdims=True)
        u = dna * gain_ref[0:1, :]
        g0_ref[...] = (
            g1_ref[...] + r * u - x * (r * r * r * jnp.mean(u * x, -1, keepdims=True))
        )
        if final:
            gn = gn + pn_ref[...]
            pick_rows(co, g0_ref, piece_refs)
        gn_ref[...] = gn

    args = [*dq, *dkv, na, h, g1, gain, w, cs, sn] + ([before] if final else [])
    shapes = [((1, width), F32)]
    if final:
        shapes = [((rows, cols), BF)] + shapes + [((width, rows // slots), BF)] * slots
    else:
        shapes = [((width, cols), F32)] + shapes + [((rows, width), F32)]
    return call(
        body,
        (1,),
        ([SMEM_SPEC] if final else []) + [whole(x.shape) for x in args],
        [whole(x) for x, _ in shapes],
        [sds(x, t) for x, t in shapes],
        [pltpu.VMEM((rows, width), F32)] if final else [],
    )(*([coords] if final else []), *args)


def qkv_weights(d, na, before):
    def body(d_ref, na_ref, pw_ref, gw_ref):
        gw_ref[...] = (dot(na_ref[...], d_ref[...], 0, 0) + pw_ref[...]).astype(BF)

    args = (d, na, before)
    return call(
        body, (1,), [whole(x.shape) for x in args], [whole(before.shape)], [sds(before.shape, BF)]
    )(*args)[0]


def shifted(total, group, step):
    pairs = []
    for i in range(total):
        z, c = divmod(i, group)
        pairs.append((i, ((z + step) % (total // group)) * group + c))
    return pairs


def within(total, group, step):
    return [(i, (i // group) * group + (i % group + step) % group) for i in range(total)]


WQ = H * HD
WK = KV * HD
COLS_A = (0, 72, 96, 120)
FOLDS = ((0, 32), (32, 32), (64, 32), (96, 32), (128, 16))
ROWS_D = 144
ROWS_F = 256
TOP = ROWS_D


def fold_out(out, cols):
    parts = []
    for start, count in FOLDS:
        part = out[start : start + count, cols]
        if count < 32:
            part = jnp.concatenate([part, jnp.zeros((32 - count, 72), part.dtype)], axis=0)
        parts.append(part)
    return jnp.concatenate(parts + [jnp.zeros((32, 24), out.dtype)], axis=1)


def pack_shards(shards):
    def body(wq, wk, wv, wo, wg, wu, wd, ga, gf, a_ref, top_ref, low_ref):
        wk_rows, wv_rows = [ref[...].astype(F32).T.astype(BF) for ref in (wk, wv)]
        a_ref[:ROWS_D, :] = jnp.concatenate(
            [wq[...], wk_rows, wv_rows, jnp.zeros((ROWS_D, 8), BF)], axis=1
        )
        row = lax.broadcasted_iota(jnp.int32, (16, 72), 0)
        ga_row = ga[...].astype(F32)
        gf_row = gf[...].astype(F32)
        gains = jnp.where(row == 0, ga_row, jnp.where(row == 1, gf_row, 0.0))
        a_ref[ROWS_D:, :] = jnp.concatenate([gains, jnp.zeros((16, 56), F32)], axis=1).astype(BF)
        wide = jnp.concatenate(
            [wg[:, :128], wu[:, :128], wg[:, 128:], wu[:, 128:]], axis=1
        )
        top_ref[...] = wide
        low_ref[:32, :] = fold_out(wo[...], slice(0, 72))
        down = jnp.concatenate(
            [wd[:, :128], wd[:, 192:320], wd[:, 128:192], wd[:, 320:]], axis=1
        ).astype(F32)
        low_ref[32:, :] = jnp.concatenate([down, jnp.zeros((8, 384), F32)], axis=0).astype(BF)

    return call(
        body,
        (1,),
        [whole(x.shape) for x in shards],
        [whole((160, 128)), whole((TOP, 384)), whole((ROWS_F - TOP, 384))],
        [sds((160, 128), BF), sds((TOP, 384), BF), sds((ROWS_F - TOP, 384), BF)],
    )(*shards)


def cross(step, count):
    return [(i, i ^ step) for i in range(count)]


def spread_z(x):
    return [x] + [lax.ppermute(x, "ctx", shifted(8, 2, d)) for d in (1, 2, 3)]


def spread_attn(pieces, mark):
    stack = jnp.stack(pieces)
    mine = [lax.ppermute(stack, "dp", cross(r, 4)) for r in (1, 2, 3)]
    mine = [stack] + after(mine, mark)
    return mine + [lax.ppermute(m, "ctx", cross(1, 8)) for m in mine]


def spread_ffn(top, low):
    top, low = jnp.stack(top), jnp.stack(low)
    top_x = lax.ppermute(top, "dp", cross(1, 4))
    low_y = lax.ppermute(low, "dp", cross(2, 4))
    top_y = lax.ppermute(top, "dp", cross(2, 4))
    low_x = lax.ppermute(low, "dp", cross(1, 4))
    top_far = lax.ppermute(top_x, "dp", cross(2, 4))
    low_far = lax.ppermute(low_y, "dp", cross(1, 4))
    mine = [top, top_x, top_y, top_far, low, low_x, low_y, low_far]
    return mine + [lax.ppermute(m, "ctx", cross(1, 8)) for m in mine]


def ordered(c, own, sibling):
    return jnp.where(c == 0, own, sibling), jnp.where(c == 0, sibling, own)


def assemble_attn(coords, arrays):
    def body(co, *refs):
        own, sib = refs[:4], refs[4:8]
        w_ref, g_ref = refs[8:]
        j_own, z_own, c_own = co[0], co[1], co[2]
        for r in range(4):
            row = pl.multiple_of((j_own ^ r) * ROWS_D, 16)
            pieces = []
            for z in range(4):
                d = lax.rem(z_own - z + 4, 4)
                pieces.extend(ordered(c_own, own[r][d], sib[r][d]))
            groups = [
                jnp.concatenate([p[:ROWS_D, a:b] for p in pieces], axis=1)
                for a, b in zip(COLS_A[:-1], COLS_A[1:])
            ]
            w_ref[pl.ds(row, ROWS_D), :] = jnp.concatenate(groups, axis=1)
            if r == 0:
                g_ref[...] = jnp.concatenate(
                    [p[ROWS_D:, :72].astype(F32) for p in pieces], axis=1
                )

    shapes = [((576, 960), BF), ((16, 576), F32)]
    return call(
        body,
        (1,),
        [SMEM_SPEC] + [whole(x.shape) for x in arrays],
        [whole(s) for s, _ in shapes],
        [sds(s, t) for s, t in shapes],
    )(coords, *arrays)


def assemble_ffn(coords, arrays):
    def body(co, *refs):
        own, sib = refs[:8], refs[8:16]
        o_ref, g_ref, u_ref, d_ref = refs[16:]
        j_own, z_own, c_own = co[0], co[1], co[2]

        def read(group, r, d):
            return jnp.concatenate([group[r][d], group[4 + r][d]], axis=0)

        for r in range(4):
            j = j_own ^ r
            row = pl.multiple_of(j * ROWS_D, 16)
            lane = pl.multiple_of(j * 384, 128)
            pieces = []
            for z in range(4):
                d = lax.rem(z_own - z + 4, 4)
                even, odd = ordered(c_own, read(own, r, d), read(sib, r, d))
                pieces.extend((even, odd))
                here = slice(384 * z, 384 * z + 384)
                for ref, first, rest in ((g_ref, 0, 256), (u_ref, 128, 320)):
                    ref[pl.ds(row, ROWS_D), here] = jnp.concatenate(
                        [
                            even[:ROWS_D, first : first + 128],
                            odd[:ROWS_D, first : first + 128],
                            even[:ROWS_D, rest : rest + 64],
                            odd[:ROWS_D, rest : rest + 64],
                        ],
                        axis=1,
                    )
                down = jnp.concatenate(
                    [even[176:248].astype(F32), odd[176:248].astype(F32)], axis=0
                )
                d_ref[ROWS_D * z : ROWS_D * z + ROWS_D, pl.ds(lane, 384)] = down.astype(BF)
            for g, (start, count) in enumerate(FOLDS):
                o_ref[pl.ds(pl.multiple_of(row + start, 16), count), :] = jnp.concatenate(
                    [p[144 : 144 + count, 72 * g : 72 * g + 72] for p in pieces], axis=1
                )

    shapes = [(576, 576), (576, 1536), (576, 1536), (576, 1536)]
    return call(
        body,
        (1,),
        [SMEM_SPEC] + [whole(x.shape) for x in arrays],
        [whole(s) for s in shapes],
        [sds(s, BF) for s in shapes],
    )(coords, *arrays)


def split_attn(coords, d_qkv, na, before, gn_attn, gn_ffn):
    def body(co, d_ref, na_ref, pw_ref, ga, gf, *outs):
        keep, away, gw = outs[:4], outs[4], outs[5]
        gw[...] = (dot(na_ref[...], d_ref[...], 0, 0) + pw_ref[...]).astype(BF)
        j_own, z_own, c_own = co[0], co[1], co[2]
        sub = lax.broadcasted_iota(jnp.int32, (16, 576), 0)
        gains = jnp.where(sub == 0, ga[...], jnp.where(sub == 1, gf[...], 0.0)).astype(BF)
        for r in range(4):
            row = pl.multiple_of((j_own ^ r) * ROWS_D, 16)
            wide = gw[pl.ds(row, ROWS_D), :]
            for z in range(4):
                d = lax.rem(z - z_own + 4, 4)
                pair = []
                for k in (2 * z, 2 * z + 1):
                    top = jnp.concatenate(
                        [
                            wide[:, 72 * k : 72 * k + 72],
                            wide[:, WQ + 24 * k : WQ + 24 * k + 24],
                            wide[:, WQ + WK + 24 * k : WQ + WK + 24 * k + 24],
                            jnp.zeros((ROWS_D, 8), BF),
                        ],
                        axis=1,
                    )
                    low = jnp.concatenate(
                        [gains[:, 72 * k : 72 * k + 72], jnp.zeros((16, 56), BF)], axis=1
                    )
                    pair.append(jnp.concatenate([top, low], axis=0))
                mine, other = ordered(c_own, *pair)
                keep[r][d] = mine
                away[r, d] = other

    shapes = [(4, 160, 128)] * 4 + [(4, 4, 160, 128)]
    args = (d_qkv, na, before, gn_attn, gn_ffn)
    return call(
        body,
        (1,),
        [SMEM_SPEC] + [whole(x.shape) for x in args],
        [whole(s) for s in shapes],
        [sds(s, BF) for s in shapes],
        [pltpu.VMEM(before.shape, BF)],
    )(coords, *args)


def split_ffn(coords, g_out, g_gate, g_up, g_down):
    def body(co, go, gg, gu, gd, *outs):
        keep, away = outs[:4], outs[4]
        j_own, z_own, c_own = co[0], co[1], co[2]
        for r in range(4):
            j = j_own ^ r
            row = pl.multiple_of(j * ROWS_D, 16)
            lane = pl.multiple_of(j * 384, 128)
            out = go[pl.ds(row, ROWS_D), :]
            for z in range(4):
                d = lax.rem(z - z_own + 4, 4)
                gate = gg[pl.ds(row, ROWS_D), 384 * z : 384 * z + 384]
                up = gu[pl.ds(row, ROWS_D), 384 * z : 384 * z + 384]
                down = gd[ROWS_D * z : ROWS_D * z + ROWS_D, pl.ds(lane, 384)].astype(F32)
                pair = []
                for i in range(2):
                    k = 2 * z + i
                    first = slice(128 * i, 128 * i + 128)
                    rest = slice(256 + 64 * i, 320 + 64 * i)
                    wide = jnp.concatenate(
                        [gate[:, first], up[:, first], gate[:, rest], up[:, rest]], axis=1
                    )
                    low = jnp.concatenate(
                        [down[72 * i : 72 * i + 72], jnp.zeros((8, 384), F32)], axis=0
                    ).astype(BF)
                    pair.append((wide, fold_out(out, slice(72 * k, 72 * k + 72)), low))
                spans = (slice(0, 144), slice(144, 176), slice(176, 256))
                for part, here in enumerate(spans):
                    mine, other = ordered(c_own, pair[0][part], pair[1][part])
                    keep[r][d, here, :] = mine
                    away[r, d, here, :] = other

    shapes = [(4, ROWS_F, 384)] * 4 + [(4, 4, ROWS_F, 384)]
    args = (g_out, g_gate, g_up, g_down)
    return call(
        body,
        (1,),
        [SMEM_SPEC] + [whole(x.shape) for x in args],
        [whole(s) for s in shapes],
        [sds(s, BF) for s in shapes],
    )(coords, *args)


def total(*terms):
    out = terms[0].astype(F32)
    for t in terms[1:]:
        out = out + t.astype(F32)
    return out.astype(BF)


def sum_z(mine):
    return [mine[0]] + [lax.ppermute(mine[d], "ctx", shifted(8, 2, d)) for d in (1, 2, 3)]


def sum_attn(pieces):
    keep, away = pieces[:4], pieces[4]
    back = lax.ppermute(away, "ctx", cross(1, 8))
    sums = [total(keep[r], back[r]) for r in (1, 2, 3)]
    moved = [lax.ppermute(x, "dp", cross(r, 4)) for r, x in zip((1, 2, 3), sums)]
    return sum_z(total(keep[0], back[0], *moved)), sums


def sum_ffn(pieces):
    keep, away = pieces[:4], pieces[4]
    back = lax.ppermute(away, "ctx", cross(1, 8))
    top, low = slice(0, TOP), slice(TOP, ROWS_F)

    def pair(r, rows, *more):
        return total(keep[r][:, rows], back[r][:, rows], *more)

    far_top, far_low = pair(3, top), pair(3, low)
    x_low, y_top = pair(1, low), pair(2, top)
    top_far = lax.ppermute(far_top, "dp", cross(2, 4))
    low_far = lax.ppermute(far_low, "dp", cross(1, 4))
    low_x = lax.ppermute(x_low, "dp", cross(1, 4))
    top_y = lax.ppermute(y_top, "dp", cross(2, 4))
    x_top, y_low = pair(1, top, top_far), pair(2, low, low_far)
    top_x = lax.ppermute(x_top, "dp", cross(1, 4))
    low_y = lax.ppermute(y_low, "dp", cross(2, 4))
    marks = (away, (far_top, far_low, x_low, y_top))

    def along_z(mark):
        moved = after((top_x, top_y, low_x, low_y), mark)
        mine = jnp.concatenate(
            [pair(0, top, moved[0], moved[1]), pair(0, low, moved[2], moved[3])], axis=1
        )
        return sum_z(mine)

    return along_z, marks


def finish(terms_f, terms_a):
    def body(*refs):
        o_ref, g_ref, u_ref, d_ref, q_ref, k_ref, v_ref, ga_ref, gf_ref = refs[8:]
        x = sum(ref[...].astype(F32) for ref in refs[4:8])
        q_ref[...] = x[:ROWS_D, :72]
        k_ref[...] = x[:ROWS_D, 72:96].T
        v_ref[...] = x[:ROWS_D, 96:120].T
        ga_ref[...] = x[ROWS_D : ROWS_D + 1, :72]
        gf_ref[...] = x[ROWS_D + 1 : ROWS_D + 2, :72]
        x = sum(ref[...].astype(F32) for ref in refs[:4])
        wide = x[:ROWS_D]
        g_ref[...] = jnp.concatenate([wide[:, :128], wide[:, 256:320]], axis=1)
        u_ref[...] = jnp.concatenate([wide[:, 128:256], wide[:, 320:]], axis=1)
        for g, (start, count) in enumerate(FOLDS):
            o_ref[start : start + count, :] = x[144 : 144 + count, 72 * g : 72 * g + 72]
        low = x[176:248]
        d_ref[...] = jnp.concatenate(
            [low[:, :128], low[:, 256:320], low[:, 128:256], low[:, 320:]], axis=1
        )

    shapes = [(ROWS_D, 72), (ROWS_D, 192), (ROWS_D, 192), (72, 384)]
    shapes += [(ROWS_D, 72), (24, ROWS_D), (24, ROWS_D), (1, 72), (1, 72)]
    terms = [*terms_f, *terms_a]
    return call(
        body,
        (1,),
        [whole(x.shape) for x in terms],
        [whole(s) for s in shapes],
        [sds(s, F32) for s in shapes],
    )(*terms)


def pick_slots(coords, x):
    slots, width, rows = x.shape

    def body(co, x_ref, *outs):
        for d in range(slots):
            outs[d][...] = x_ref[lax.rem(co[1] + d, slots)]

    return call(
        body,
        (1,),
        [SMEM_SPEC, whole(x.shape)],
        [whole((width, rows))] * slots,
        [sds((width, rows), BF)] * slots,
    )(coords, x)


def place_slots(coords, pieces, dtype):
    slots = len(pieces)
    width, rows = pieces[0].shape

    def body(co, *refs):
        for d in range(slots):
            refs[slots][lax.rem(co[1] - d + slots, slots)] = refs[d][...].astype(dtype)

    return call(
        body,
        (1,),
        [SMEM_SPEC] + [whole((width, rows))] * slots,
        [whole((slots, width, rows))],
        [sds((slots, width, rows), dtype)],
    )(coords, *pieces)[0]


def redeal(pieces, ctx, group):
    return [pieces[0]] + [
        lax.ppermute(pieces[d], "ctx", shifted(ctx, group, d))
        for d in range(1, len(pieces))
    ]


def exchange(kv, ctx, group):
    return [kv] + [lax.ppermute(kv, "ctx", within(ctx, group, e)) for e in range(1, group)]


def after(x, mark):
    return lax.optimization_barrier((x, mark))[0]


def tables(slots, block, group):
    c = lax.axis_index("ctx") % group
    half_width = HD // 2
    frequency = jnp.exp(jnp.arange(half_width, dtype=F32) * (-2.0 * math.log(10000.0) / HD))
    positions = (group * jnp.arange(slots)[:, None] + c) * block + jnp.arange(block)[None, :]
    angles = positions.reshape(-1).astype(F32)[:, None] * frequency[None, :]
    cosine, sine = jnp.cos(angles), jnp.sin(angles)
    return (
        jnp.concatenate([cosine] * 4, axis=1),
        jnp.concatenate([-sine, sine, -sine, sine], axis=1),
    )


def gather_matrix(shard):
    return lax.all_gather(
        lax.all_gather(shard, "ctx", axis=1, tiled=True), "dp", axis=0, tiled=True
    )


def scatter_matrix(grad):
    part = lax.psum_scatter(grad, "dp", scatter_dimension=0, tiled=True)
    return lax.psum_scatter(part, "ctx", scatter_dimension=1, tiled=True).astype(F32)


def step(
    tokens,
    prefix,
    norm_attn,
    w_query,
    w_key,
    w_value,
    w_output,
    norm_ffn,
    w_gate,
    w_up,
    w_down,
    cotangent,
):
    slots, _, block, width = tokens.shape
    ctx = lax.axis_size("ctx")
    group = ctx // slots
    index = lax.axis_index("ctx")
    c = index % group
    cs, sn = tables(slots, block, group)
    micro_prefix = lax.dynamic_index_in_dim(prefix[:, 0], index // group, 0, keepdims=True)
    members = (c - jnp.arange(group)) % group
    meta = jnp.concatenate([micro_prefix, members]).astype(jnp.int32)

    dp = lax.axis_size("dp")
    coords = jnp.stack([lax.axis_index("dp"), index // group, c]).astype(jnp.int32)
    tight = dp == 4 and ctx == 8 and slots == 4 and w_query.shape == (ROWS_D, 72)

    own_tokens = jnp.swapaxes(tokens[:, 0], 1, 2)
    if tight:
        shards = (w_query, w_key.T, w_value.T, w_output, w_gate, w_up, w_down.T)
        pack_a, pack_top, pack_low = pack_shards(shards + (norm_attn[None], norm_ffn[None]))
        stack_a = spread_z(pack_a)
        picked = pick_slots(coords, after(own_tokens, pack_a))
        h = redeal(picked, ctx, group)
        w_qkv, gains = assemble_attn(coords, spread_attn(stack_a, (cs, sn, meta)))
        spread = spread_ffn(spread_z(pack_top), spread_z(pack_low))
        w_out, *w_ffn = assemble_ffn(coords, spread)
    else:
        gains = lax.all_gather(jnp.stack([norm_attn, norm_ffn]), "ctx", axis=1, tiled=True)
        gains = jnp.concatenate([gains.astype(F32), jnp.zeros((14, width), F32)], axis=0)
        w_qkv = jnp.concatenate(
            [gather_matrix(w_query), gather_matrix(w_key), gather_matrix(w_value)], axis=1
        )
        h = redeal(pick_slots(coords, own_tokens), ctx, group)
        w_out = gather_matrix(w_output)
        w_ffn = [gather_matrix(w_gate), gather_matrix(w_up), gather_matrix(w_down).T]
    full = (w_out, gains, *w_ffn)

    kept = []
    for layer in range(2):
        last = layer == 1
        na, q, kv, *dealt = qkv_forward(h, gains, w_qkv, cs, sn, None if last else coords)
        if dealt:
            h = dealt[0]
        kv_parts = exchange(kv, ctx, group)
        att, linv, *probs = attend_forward(q, kv_parts, meta, slots)
        h1, nb, a, b, hid, h2, *out_pieces = ffn_forward(
            h, att, *full, coords if last else None, slots
        )
        kept.append((h, na, q, kv_parts, att, linv, probs, h1, nb, a, b, hid))
        h = h2

    g = pick_slots(coords, jnp.swapaxes(cotangent[:, 0], 1, 2))
    g = redeal(g, ctx, group)
    out_pieces = redeal(out_pieces, ctx, group)
    block_output = place_slots(coords, out_pieces, BF)
    before_ffn = None
    for layer in (1, 0):
        h, na, q, kv_parts, att, linv, probs, h1, nb, a, b, hid = kept[layer]
        *before_ffn, g1, datt = ffn_backward(
            g, (h1, nb, a, b, hid, att), full, before_ffn, coords if layer == 1 else None
        )
        back_args = (q, kv_parts, datt, att, linv, probs, cs, sn, slots)
        chunks = [(0, KV)]
        if layer == 0 and tight:
            grad_down, grad_gate, grad_up, grad_out, gn_ffn = before_ffn
            parts_f = split_ffn(coords, grad_out, grad_gate, grad_up, grad_down)
            along_z, marks = sum_ffn(parts_f)
        dq, sent = [], []
        for n, (first, count) in enumerate(chunks):
            args = back_args
            if layer == 0 and tight:
                args = (after(q, marks[n]),) + back_args[1:]
            got = attend_backward(*args, first, count)
            dq.append(got[0])
            sent.append(got[1:])
        own = [parts[0] for parts in sent]
        moved = [
            lax.ppermute(parts[e], "ctx", within(ctx, group, -e))
            for e in range(1, group)
            for parts in sent
        ]
        dkv = own + moved
        back = (dq, dkv, na, h, g1, gains, w_qkv, cs, sn)
        if layer == 1:
            before_qkv, gn_attn, g = qkv_backward(*back, None)
        else:
            d_qkv, gn_attn, *g = qkv_backward(*back, gn_attn, coords, slots)
    input_grad = place_slots(coords, redeal(g, ctx, group), F32)
    grad_down, grad_gate, grad_up, grad_out, gn_ffn = before_ffn
    if tight:
        split = split_attn(coords, d_qkv, na, before_qkv, gn_attn, gn_ffn)
        terms_a, sums_a = sum_attn(split)
        done = finish(along_z(sums_a), terms_a)
        g_out, g_gate, g_up, g_down, g_query, g_key, g_value, gn_attn, gn_ffn = done
        g_key, g_value, g_down = g_key.T, g_value.T, g_down.T
        gn = (gn_attn[0], gn_ffn[0])
    else:
        gn = lax.psum(jnp.concatenate([gn_attn, gn_ffn], axis=0), "dp")
        gn = lax.psum_scatter(gn, "ctx", scatter_dimension=1, tiled=True)
        grad_qkv = qkv_weights(d_qkv, na, before_qkv)
        g_query = scatter_matrix(grad_qkv[:, :WQ])
        g_key = scatter_matrix(grad_qkv[:, WQ : WQ + WK])
        g_value = scatter_matrix(grad_qkv[:, WQ + WK :])
        g_out = scatter_matrix(grad_out)
        g_gate, g_up, g_down = [scatter_matrix(x) for x in (grad_gate, grad_up, grad_down.T)]
    return (
        jnp.swapaxes(block_output, 1, 2)[:, None],
        jnp.swapaxes(input_grad, 1, 2)[:, None],
        gn[0],
        g_query,
        g_key,
        g_value,
        g_out,
        gn[1],
        g_gate,
        g_up,
        g_down,
    )


def solution(mesh):
    act = P(None, "dp", "ctx", None)
    mat = P("dp", "ctx")
    in_specs = (act, P(None, "dp"), P("ctx"), mat, mat, mat, mat, P("ctx"), mat, mat, mat, act)
    out_specs = (act, act, P("ctx"), mat, mat, mat, mat, P("ctx"), mat, mat, mat)
    return jax.shard_map(step, mesh=mesh, in_specs=in_specs, out_specs=out_specs, check_vma=False)
```
